128 devices in a mesh: head: 16 (over y, z_hi, core), tail: 8 (over z_lo, x).
Axes of the slice: x: 4, y: 4, z: 4 (z_hi: 2, z_lo: 2; z = z_hi * 2 + z_lo), core: 2. Of those that a mesh axis runs over, the one named last changes fastest.
Arguments:
- head_emb: float32 [16, 512, 256], P('head'), may hold values from -1.5 to 1.5
- tail_emb: float32 [8, 2048, 256], P('tail'), may hold values from -1.5 to 1.5
- relations: float32 [4096, 256], P(('head', 'tail')), may hold values from -0.375 to 0.375
- head_index: int32 [16, 8, 2, 1, 512], P('head', 'tail'), may hold values from 0 to 511
- tail_index: int32 [16, 8, 2, 1, 512], P('head', 'tail'), may hold values from 0 to 2047
- rel_index: int32 [16, 8, 2, 1, 512], P('head', 'tail'), may hold values from 0 to 15
- neg_index: int32 [16, 8, 2, 1, 512], P('head', 'tail'), may hold values from 0 to 2047
Outputs:
- head_grad: float32 [16, 512, 256], P('head', 'tail')
- tail_grad: float32 [8, 2048, 256], P('tail', 'head')
- rel_grad: float32 [4096, 256], P(('head', 'tail'))
The draws below stay inside these ranges and needn't reach their ends.
All inputs are finite; a program needn't handle non-finite values.
Results may differ from the reference program's by a relative error of at most 0.00028.
Values sent between devices are 32-bit elements; how exact they have to be, the bound alone decides.
No kernel may reach another device: no remote copies, remote signals or barrier semaphores. Data moves between devices by JAX's collectives and lax.ppermute only.
A program may use at most 128 MiB of HBM per device.

```python
import math
import jax
import jax.numpy as jnp
import numpy as np
from jax import lax

D = 256
NREL = 16
B = 512
NEG = 512
STEPS = 2
BLOCKS = 1
EH = 512
ET = 2048
N_HEAD = 16
N_TAIL = 8


def place_ends(values, key, least, top_value):
    index_at = [jax.random.randint(jax.random.fold_in(key, axis), (), 0, length) for axis, length in enumerate(values.shape)]
    widest = values.shape.index(max(values.shape))
    beside = index_at[:widest] + [(index_at[widest] + 1) % values.shape[widest]] + index_at[widest + 1:]
    return values.at[tuple(index_at)].set(least).at[tuple(beside)].set(top_value)


def levels(key, extent, shards, low, high):
    def one(dim, shards_of):
        steps = jax.random.uniform(jax.random.fold_in(jax.random.fold_in(key, 6), dim), (shards_of,), jnp.float32, low / len(shards), high / len(shards))
        return jnp.repeat(jnp.exp(steps), extent[dim] // shards_of).reshape((-1,) + (1,) * (len(extent) - dim - 1))

    loudness = one(*shards[0])
    for cut in shards[1:]:
        loudness = loudness * one(*cut)
    return loudness


def cumulative_ranks(amount, slope):
    weights = [(1 << 20) // math.isqrt(rank ** slope) + 1 for rank in range(1, amount + 1)]
    width = 1 + sum(weights) // (1 << 30)
    return np.cumsum(np.array([max(1, weight // width) for weight in weights]))


def skewed_ids(rng, extent, count, lean):
    listing = cumulative_ranks(count, lean)
    ticket = jax.random.randint(jax.random.fold_in(rng, 1), extent, 0, int(listing[count - 1]))
    grade = jnp.searchsorted(jnp.asarray(listing, jnp.int32), ticket, side="right")
    return jax.random.permutation(jax.random.fold_in(rng, 2), count)[grade].astype(jnp.int32)


def scatter_about(rng, dims, scale, limit, cuts=(), held_as=jnp.bfloat16):
    level = levels(rng, dims, cuts, -0.22, 0.18) if cuts else 1.0
    entries = jax.random.normal(rng, dims, jnp.float32) * scale * level
    return jnp.minimum(jnp.maximum(entries, -limit), limit).astype(held_as)


def setup_inputs(seed: int = 0) -> dict:
    streams_of = jax.random.split(jax.random.key(seed), 8)
    return {
        "head_emb": scatter_about(streams_of[0], (N_HEAD, EH, D), 0.25, 1.5, ((0, 16),), jnp.float32),
        "tail_emb": scatter_about(streams_of[1], (N_TAIL, ET, D), 0.25, 1.5, ((0, 8),), jnp.float32),
        "relations": scatter_about(streams_of[2], (NREL * D, D), D ** -0.5, 0.375, ((0, 128),), jnp.float32),
        "head_index": place_ends(jax.random.randint(streams_of[3], (N_HEAD, N_TAIL, STEPS, BLOCKS, B), 0, EH), jax.random.fold_in(streams_of[3], 1), 0, EH - 1).astype(jnp.int32),
        "tail_index": place_ends(jax.random.randint(streams_of[4], (N_HEAD, N_TAIL, STEPS, BLOCKS, B), 0, ET), jax.random.fold_in(streams_of[4], 1), 0, ET - 1).astype(jnp.int32),
        "rel_index": place_ends(skewed_ids(streams_of[5], (N_HEAD, N_TAIL, STEPS, BLOCKS, B), NREL, 2), jax.random.fold_in(streams_of[5], 3), 0, NREL - 1).astype(jnp.int32),
        "neg_index": place_ends(jax.random.randint(streams_of[6], (N_HEAD, N_TAIL, STEPS, BLOCKS, NEG), 0, ET), jax.random.fold_in(streams_of[6], 1), 0, ET - 1).astype(jnp.int32),
    }


def reference(head_emb, tail_emb, relations, head_index, tail_index, rel_index, neg_index):
    highest = lax.Precision.HIGHEST
    rel_mats = relations.reshape(NREL, D, D)
    head_part = jnp.broadcast_to(jnp.arange(N_HEAD, dtype=jnp.int32)[:, None, None, None], (N_HEAD, N_TAIL, STEPS, BLOCKS))
    group = jnp.arange(N_TAIL, dtype=jnp.int32)[None, :, None, None]
    stepno = jnp.arange(STEPS, dtype=jnp.int32)[None, None, :, None]
    tail_part = jnp.broadcast_to((group - stepno) % N_TAIL, (N_HEAD, N_TAIL, STEPS, BLOCKS)).astype(jnp.int32)
    inputs = (head_part.reshape(-1), tail_part.reshape(-1), head_index.reshape(-1, B), tail_index.reshape(-1, B), rel_index.reshape(-1, B), neg_index.reshape(-1, NEG))

    def one_block(carry, items):
        grad_head, grad_tail, grad_rel = carry
        part_h, part_t, rows_h, rows_t, rows_r, rows_n = items
        head_vec = head_emb[part_h][rows_h]
        tail_vec = tail_emb[part_t][rows_t]
        negatives = tail_emb[part_t][rows_n]
        chosen = rel_mats[rows_r]
        query = jnp.einsum("bd,bde->be", head_vec, chosen, precision=highest)
        positive = jnp.sum(query * tail_vec, axis=1)
        negative = jnp.dot(query, negatives.T, precision=highest)
        coef = -jax.nn.sigmoid(-positive)
        weights = jax.nn.sigmoid(negative) / NEG
        factor = coef[:, None] * tail_vec + jnp.dot(weights, negatives, precision=highest)
        back = jnp.einsum("bde,be->bd", chosen, factor, precision=highest)
        grad_head = grad_head.at[part_h, rows_h].add(back)
        grad_tail = grad_tail.at[part_t, rows_t].add(coef[:, None] * query)
        grad_tail = grad_tail.at[part_t, rows_n].add(jnp.dot(weights.T, query, precision=highest))
        outer = jnp.einsum("bd,be->bde", head_vec, factor)
        grad_rel = grad_rel.at[rows_r].add(outer)
        return (grad_head, grad_tail, grad_rel), None

    start = (jnp.zeros((N_HEAD, EH, D), jnp.float32), jnp.zeros((N_TAIL, ET, D), jnp.float32), jnp.zeros((NREL, D, D), jnp.float32))
    (grad_head, grad_tail, grad_rel), unused = lax.scan(one_block, start, inputs)
    return grad_head, grad_tail, grad_rel.reshape(NREL * D, D)
```

```python
import functools

import jax
import jax.numpy as jnp
from jax import lax
from jax.experimental import pallas as pl
from jax.experimental.pallas import tpu as pltpu
from jax.sharding import Mesh, PartitionSpec as P

BF = jnp.bfloat16
F32 = jnp.float32
CHIPS = ("y", "zh", "zl", "x")
HEAD = ("y", "zh", "c")
HEAD_CHIPS = ("y", "zh")
TAIL = ("zl", "x")
SWAP = [(0, 1), (1, 0)]
VMEM_LIMIT = 60 << 20
NN = (((1,), (0,)), ((), ()))
NT = (((1,), (1,)), ((), ()))
TN = (((0,), (0,)), ((), ()))


def split(value):
    high = value.astype(BF)
    return high, (value - high.astype(F32)).astype(BF)


def dot(a, b, dims=NN):
    return lax.dot_general(a, b, dims, preferred_element_type=F32)


def dot3(a, b, dims=NN):
    return dot(a[0], b[0], dims) + dot(a[0], b[1], dims) + dot(a[1], b[0], dims)


def ones_where(mask):
    return jnp.where(mask, 1.0, 0.0).astype(BF)


def call(body, out_shape, scratch, args, smem=0):
    in_specs = [pl.BlockSpec(memory_space=pltpu.SMEM)] * smem
    in_specs += [pl.BlockSpec(memory_space=pltpu.VMEM)] * (len(args) - smem)
    return pl.pallas_call(
        body,
        out_shape=out_shape,
        in_specs=in_specs,
        out_specs=jax.tree.map(lambda _: pl.BlockSpec(memory_space=pltpu.VMEM), out_shape),
        scratch_shapes=scratch,
        compiler_params=pltpu.CompilerParams(vmem_limit_bytes=VMEM_LIMIT),
    )(*args)


def gather_body(cols, head, tail, hv_hi, hv_lo, hvt_hi, hvt_lo, tv, n_hi, n_lo, head_hl, tail_hl):
    width = head.shape[1]
    high, low = split(head[...])
    head_hl[:, :width] = high
    head_hl[:, width:] = low
    high, low = split(tail[...])
    tail_hl[:, :width] = high
    tail_hl[:, width:] = low
    step = 256

    def chunk(i, carry):
        rows = pl.ds(pl.multiple_of(i * step, step), step)
        part = cols[rows, :]

        def pick(column, table):
            count = table.shape[0]
            ids = lax.broadcasted_iota(jnp.int32, (step, count), 1)
            return dot(ones_where(part[:, column : column + 1] == ids), table[...])

        both = pick(0, head_hl)
        high, low = both[:, :width], both[:, width:]
        hv_hi[rows, :] = high.astype(BF)
        hv_lo[rows, :] = low.astype(BF)
        hvt_hi[:, rows] = jnp.transpose(high).astype(BF)
        hvt_lo[:, rows] = jnp.transpose(low).astype(BF)
        both = pick(1, tail_hl)
        tv[rows, :] = both[:, :width] + both[:, width:]
        both = pick(3, tail_hl)
        n_hi[rows, :] = both[:, :width].astype(BF)
        n_lo[rows, :] = both[:, width:].astype(BF)
        return carry

    lax.fori_loop(0, cols.shape[0] // step, chunk, 0)


def rel_id(core, half, j):
    return 2 * j + (core if half == 0 else 1 - core)


def factor_body(core_ref, cols, hv_hi, hv_lo, tv, n_hi, n_lo, own, other, f_hi, f_lo, d_hl, query):
    core = core_ref[0]
    width = own.shape[1]
    rels = cols[:, 2:3]
    query[...] = jnp.zeros_like(query)

    def one(j, carry):
        rows = pl.ds(pl.multiple_of(j * width, width), width)
        total = query[...]
        for half, mats in ((0, own), (1, other)):
            mask = ones_where(rels == rel_id(core, half, j))
            total += dot3((hv_hi[...] * mask, hv_lo[...] * mask), split(mats[rows, :]))
        query[...] = total
        return carry

    lax.fori_loop(0, own.shape[0] // width, one, 0)
    triples = cols.shape[0]
    batch = triples // 2
    for s in range(2):
        rows = slice(s * batch, (s + 1) * batch)
        q = query[rows, :]
        q2 = split(q)
        n2 = (n_hi[rows, :], n_lo[rows, :])
        weights = split(jax.nn.sigmoid(dot3(q2, n2, NT)) * (1.0 / batch))
        vec = tv[rows, :]
        coef = -jax.nn.sigmoid(-jnp.sum(q * vec, axis=1, keepdims=True))
        high, low = split(coef * vec + dot3(weights, n2))
        f_hi[rows, :] = high
        f_lo[rows, :] = low
        high, low = split(coef * q)
        d_hl[rows, :width] = high
        d_hl[rows, width:] = low
        high, low = split(dot3(weights, q2, TN))
        below = slice(triples + s * batch, triples + (s + 1) * batch)
        d_hl[below, :width] = high
        d_hl[below, width:] = low


def rel_body(half, core_ref, rows_ref, hvt_hi, hvt_lo, f_hi, f_lo, out):
    core = core_ref[0]
    width = f_hi.shape[1]
    rels = rows_ref[2:3, :]

    def one(j, carry):
        mask = ones_where(rels == rel_id(core, half, j))
        rows = pl.ds(pl.multiple_of(j * width, width), width)
        out[rows, :] = dot3((hvt_hi[...] * mask, hvt_lo[...] * mask), (f_hi[...], f_lo[...]))
        return carry

    lax.fori_loop(0, out.shape[0] // width, one, 0)


def tail_body(core_ref, rows_ref, d_hl, mine, theirs):
    core = core_ref[0]
    width = mine.shape[1]
    ids = jnp.concatenate([rows_ref[1:2, :], rows_ref[3:4, :]], axis=1)
    step = 512
    block = 128

    for half, out in ((0, mine), (1, theirs)):
        parity = rel_id(core, half, 0)

        def chunk(i, carry, parity=parity, out=out):
            place = i * step + lax.broadcasted_iota(jnp.int32, (step, ids.shape[1]), 0)
            row = (place // block) * (2 * block) + parity * block + place % block
            both = dot(ones_where(row == ids), d_hl[...])
            rows = pl.ds(pl.multiple_of(i * step, step), step)
            out[rows, :] = both[:, :width] + both[:, width:]
            return carry

        lax.fori_loop(0, out.shape[0] // step, chunk, 0)


def head_body(core_ref, cols, rows_ref, f_hi, f_lo, own, other, out, through, th_hl):
    core = core_ref[0]
    width = own.shape[1]
    rels = cols[:, 2:3]
    through[...] = jnp.zeros_like(through)

    def one(j, carry):
        rows = pl.ds(pl.multiple_of(j * width, width), width)
        total = through[...]
        for half, mats in ((0, own), (1, other)):
            mask = ones_where(rels == rel_id(core, half, j))
            total += dot3((f_hi[...] * mask, f_lo[...] * mask), split(mats[rows, :]), NT)
        through[...] = total
        return carry

    lax.fori_loop(0, own.shape[0] // width, one, 0)
    high, low = split(through[...])
    th_hl[:, :width] = high
    th_hl[:, width:] = low
    ids = rows_ref[0:1, :]
    place = lax.broadcasted_iota(jnp.int32, (out.shape[0], ids.shape[1]), 0)
    both = dot(ones_where(place == ids), th_hl[...])
    out[...] = both[:, :width] + both[:, width:]


def shape(*dims, dtype=F32):
    return jax.ShapeDtypeStruct(dims, dtype)


def exchange_sum(value, axes):
    devices = lax.axis_size(axes)
    pieces = value.reshape(devices, value.shape[0] // devices, value.shape[1])
    return jnp.sum(lax.all_to_all(pieces, axes, split_axis=0, concat_axis=0), axis=0)


def per_device(head_emb, tail_emb, relations, head_index, tail_index, rel_index, neg_index):
    width = relations.shape[1]
    heads = head_emb[0]
    tails = tail_emb[0]
    batch = head_index.shape[4]
    triples = 2 * batch
    index = jnp.stack([a[0, 0, :, 0] for a in (head_index, tail_index, rel_index, neg_index)], axis=1)
    behind = lax.axis_size(TAIL)
    next_index = lax.ppermute(index[1], TAIL, [(i, (i - 1) % behind) for i in range(behind)])
    rows = jnp.concatenate([index[0], next_index], axis=1)
    cols = jnp.transpose(rows)
    core = lax.axis_index("c").astype(jnp.int32).reshape(1)

    chips = lax.axis_size(CHIPS)
    spread = jnp.broadcast_to(relations[None], (chips,) + relations.shape)
    own = lax.all_to_all(spread, CHIPS, split_axis=0, concat_axis=0).reshape(-1, width)
    other = lax.ppermute(own, "c", SWAP)

    hv_hi, hv_lo, hvt_hi, hvt_lo, tv, n_hi, n_lo = call(
        gather_body,
        [shape(triples, width, dtype=BF)] * 2
        + [shape(width, triples, dtype=BF)] * 2
        + [shape(triples, width)]
        + [shape(triples, width, dtype=BF)] * 2,
        [pltpu.VMEM((heads.shape[0], 2 * width), BF), pltpu.VMEM((tails.shape[0], 2 * width), BF)],
        (cols, heads, tails),
    )
    f_hi, f_lo, d_hl = call(
        factor_body,
        [shape(triples, width, dtype=BF)] * 2 + [shape(2 * triples, 2 * width, dtype=BF)],
        [pltpu.VMEM((triples, width), F32)],
        (core, cols, hv_hi, hv_lo, tv, n_hi, n_lo, own, other),
        smem=1,
    )
    rel_args = (core, rows, hvt_hi, hvt_lo, f_hi, f_lo)
    rel_other = call(functools.partial(rel_body, 1), shape(*own.shape), [], rel_args, smem=1)
    rel_own = call(functools.partial(rel_body, 0), shape(*own.shape), [], rel_args, smem=1)
    rel_share = exchange_sum(rel_own + lax.ppermute(rel_other, "c", SWAP), CHIPS)

    tail_mine, tail_theirs = call(
        tail_body, [shape(tails.shape[0] // 2, width)] * 2, [], (core, rows, d_hl), smem=1
    )
    tail_share = exchange_sum(tail_mine + lax.ppermute(tail_theirs, "c", SWAP), HEAD_CHIPS)

    head_grad = call(
        head_body,
        shape(*heads.shape),
        [pltpu.VMEM((triples, width), F32), pltpu.VMEM((triples, 2 * width), BF)],
        (core, cols, rows, f_hi, f_lo, own, other),
        smem=1,
    )
    head_share = exchange_sum(head_grad, TAIL)
    return (head_share[None], tail_share[None], rel_share)


def solution(mesh):
    fine = Mesh(mesh.devices.reshape(4, 2, 2, 2, 4), ("y", "zh", "c", "zl", "x"))
    placed = (
        P(HEAD, None, None),
        P(TAIL, None, None),
        P(HEAD + TAIL, None),
        P(HEAD, TAIL, None, None, None),
        P(HEAD, TAIL, None, None, None),
        P(HEAD, TAIL, None, None, None),
        P(HEAD, TAIL, None, None, None),
    )
    return jax.shard_map(
        per_device,
        mesh=fine,
        in_specs=placed,
        out_specs=(P(HEAD, TAIL, None), P(TAIL, HEAD, None), P(HEAD + TAIL, None)),
        check_vma=False,
    )
```

```python
import functools

import jax
import jax.numpy as jnp
from jax import lax
from jax.experimental import pallas as pl
from jax.experimental.pallas import tpu as pltpu
from jax.sharding import Mesh, PartitionSpec as P

BF = jnp.bfloat16
F32 = jnp.float32
CHIPS = ("y", "zh", "zl", "x")
HEAD = ("y", "zh", "c")
HEAD_CHIPS = ("y", "zh")
TAIL = ("zl", "x")
SWAP = [(0, 1), (1, 0)]
VMEM_LIMIT = 60 << 20
NN = (((1,), (0,)), ((), ()))
NT = (((1,), (1,)), ((), ()))
TN = (((0,), (0,)), ((), ()))


def split(value):
    high = value.astype(BF)
    return high, (value - high.astype(F32)).astype(BF)


def dot(a, b, dims=NN):
    return lax.dot_general(a, b, dims, preferred_element_type=F32)


def dot3(a, b, dims=NN):
    return dot(a[0], b[0], dims) + dot(a[0], b[1], dims) + dot(a[1], b[0], dims)


def ones_where(mask):
    return jnp.where(mask, 1.0, 0.0).astype(BF)


def call(body, out_shape, scratch, args, smem=0):
    in_specs = [pl.BlockSpec(memory_space=pltpu.SMEM)] * smem
    in_specs += [pl.BlockSpec(memory_space=pltpu.VMEM)] * (len(args) - smem)
    return pl.pallas_call(
        body,
        out_shape=out_shape,
        in_specs=in_specs,
        out_specs=jax.tree.map(lambda _: pl.BlockSpec(memory_space=pltpu.VMEM), out_shape),
        scratch_shapes=scratch,
        compiler_params=pltpu.CompilerParams(vmem_limit_bytes=VMEM_LIMIT),
    )(*args)


def gather_body(cols, head, tail, hv_hi, hv_lo, hvt_hi, hvt_lo, tv, n_hi, n_lo, head_hl, tail_hl):
    width = head.shape[1]
    high, low = split(head[...])
    head_hl[:, :width] = high
    head_hl[:, width:] = low
    high, low = split(tail[...])
    tail_hl[:, :width] = high
    tail_hl[:, width:] = low
    step = 256

    def chunk(i, carry):
        rows = pl.ds(pl.multiple_of(i * step, step), step)
        part = cols[rows, :]

        def pick(column, table):
            count = table.shape[0]
            ids = lax.broadcasted_iota(jnp.int32, (step, count), 1)
            return dot(ones_where(part[:, column : column + 1] == ids), table[...])

        both = pick(0, head_hl)
        high, low = both[:, :width], both[:, width:]
        hv_hi[rows, :] = high.astype(BF)
        hv_lo[rows, :] = low.astype(BF)
        hvt_hi[:, rows] = jnp.transpose(high).astype(BF)
        hvt_lo[:, rows] = jnp.transpose(low).astype(BF)
        both = pick(1, tail_hl)
        tv[rows, :] = both[:, :width] + both[:, width:]
        both = pick(3, tail_hl)
        n_hi[rows, :] = both[:, :width].astype(BF)
        n_lo[rows, :] = both[:, width:].astype(BF)
        return carry

    lax.fori_loop(0, cols.shape[0] // step, chunk, 0)


def rel_id(core, half, j):
    return 2 * j + (core if half == 0 else 1 - core)


def add_query(half, core_ref, cols, hv_hi, hv_lo, mats, query):
    core = core_ref[0]
    width = mats.shape[1]
    rels = cols[:, 2:3]

    def one(j, carry):
        rows = pl.ds(pl.multiple_of(j * width, width), width)
        mask = ones_where(rels == rel_id(core, half, j))
        query[...] += dot3((hv_hi[...] * mask, hv_lo[...] * mask), split(mats[rows, :]))
        return carry

    lax.fori_loop(0, mats.shape[0] // width, one, 0)


def query_body(half, core_ref, cols, hv_hi, hv_lo, mats, query):
    query[...] = jnp.zeros_like(query)
    add_query(half, core_ref, cols, hv_hi, hv_lo, mats, query)


def factor_body(core_ref, cols, hv_hi, hv_lo, tv, n_hi, n_lo, partial, other, f_hi, f_lo, d_hl, query):
    width = other.shape[1]
    query[...] = partial[...]
    add_query(1, core_ref, cols, hv_hi, hv_lo, other, query)
    triples = cols.shape[0]
    batch = triples // 2
    for s in range(2):
        rows = slice(s * batch, (s + 1) * batch)
        q = query[rows, :]
        q2 = split(q)
        n2 = (n_hi[rows, :], n_lo[rows, :])
        weights = split(jax.nn.sigmoid(dot3(q2, n2, NT)) * (1.0 / batch))
        vec = tv[rows, :]
        coef = -jax.nn.sigmoid(-jnp.sum(q * vec, axis=1, keepdims=True))
        high, low = split(coef * vec + dot3(weights, n2))
        f_hi[rows, :] = high
        f_lo[rows, :] = low
        high, low = split(coef * q)
        d_hl[rows, :width] = high
        d_hl[rows, width:] = low
        high, low = split(dot3(weights, q2, TN))
        below = slice(triples + s * batch, triples + (s + 1) * batch)
        d_hl[below, :width] = high
        d_hl[below, width:] = low


def rel_body(half, core_ref, rows_ref, hvt_hi, hvt_lo, f_hi, f_lo, out):
    core = core_ref[0]
    width = f_hi.shape[1]
    rels = rows_ref[2:3, :]

    def one(j, carry):
        mask = ones_where(rels == rel_id(core, half, j))
        rows = pl.ds(pl.multiple_of(j * width, width), width)
        out[rows, :] = dot3((hvt_hi[...] * mask, hvt_lo[...] * mask), (f_hi[...], f_lo[...]))
        return carry

    lax.fori_loop(0, out.shape[0] // width, one, 0)


def tail_body(core_ref, rows_ref, d_hl, mine, theirs):
    core = core_ref[0]
    width = mine.shape[1]
    ids = jnp.concatenate([rows_ref[1:2, :], rows_ref[3:4, :]], axis=1)
    step = 512
    block = 128

    for half, out in ((0, mine), (1, theirs)):
        parity = rel_id(core, half, 0)

        def chunk(i, carry, parity=parity, out=out):
            place = i * step + lax.broadcasted_iota(jnp.int32, (step, ids.shape[1]), 0)
            row = (place // block) * (2 * block) + parity * block + place % block
            both = dot(ones_where(row == ids), d_hl[...])
            rows = pl.ds(pl.multiple_of(i * step, step), step)
            out[rows, :] = both[:, :width] + both[:, width:]
            return carry

        lax.fori_loop(0, out.shape[0] // step, chunk, 0)


def head_body(core_ref, cols, rows_ref, f_hi, f_lo, own, other, out, through, th_hl):
    core = core_ref[0]
    width = own.shape[1]
    rels = cols[:, 2:3]
    through[...] = jnp.zeros_like(through)

    def one(j, carry):
        rows = pl.ds(pl.multiple_of(j * width, width), width)
        total = through[...]
        for half, mats in ((0, own), (1, other)):
            mask = ones_where(rels == rel_id(core, half, j))
            total += dot3((f_hi[...] * mask, f_lo[...] * mask), split(mats[rows, :]), NT)
        through[...] = total
        return carry

    lax.fori_loop(0, own.shape[0] // width, one, 0)
    high, low = split(through[...])
    th_hl[:, :width] = high
    th_hl[:, width:] = low
    ids = rows_ref[0:1, :]
    place = lax.broadcasted_iota(jnp.int32, (out.shape[0], ids.shape[1]), 0)
    both = dot(ones_where(place == ids), th_hl[...])
    out[...] = both[:, :width] + both[:, width:]


def shape(*dims, dtype=F32):
    return jax.ShapeDtypeStruct(dims, dtype)


def exchange_sum(value, axes):
    devices = lax.axis_size(axes)
    pieces = value.reshape(devices, value.shape[0] // devices, value.shape[1])
    return jnp.sum(lax.all_to_all(pieces, axes, split_axis=0, concat_axis=0), axis=0)


def permute_sum(value, axes):
    devices = lax.axis_size(axes)
    me = lax.axis_index(axes)
    pieces = value.reshape(devices, value.shape[0] // devices, value.shape[1])
    total = lax.dynamic_index_in_dim(pieces, me, 0, keepdims=False)
    for k in range(1, devices):
        piece = lax.dynamic_index_in_dim(pieces, me ^ k, 0, keepdims=False)
        total += lax.ppermute(piece, axes, [(i, i ^ k) for i in range(devices)])
    return total


def per_device(head_emb, tail_emb, relations, head_index, tail_index, rel_index, neg_index):
    width = relations.shape[1]
    heads = head_emb[0]
    tails = tail_emb[0]
    batch = head_index.shape[4]
    triples = 2 * batch
    index = jnp.stack([a[0, 0, :, 0] for a in (head_index, tail_index, rel_index, neg_index)], axis=1)
    behind = lax.axis_size(TAIL)
    next_index = lax.ppermute(index[1], TAIL, [(i, (i - 1) % behind) for i in range(behind)])
    core = lax.axis_index("c").astype(jnp.int32).reshape(1)

    chips = lax.axis_size(CHIPS)
    spread = jnp.broadcast_to(relations[None], (chips,) + relations.shape)
    spread, next_index = lax.optimization_barrier((spread, next_index))
    rows = jnp.concatenate([index[0], next_index], axis=1)
    cols = jnp.transpose(rows)
    own = lax.all_to_all(spread, CHIPS, split_axis=0, concat_axis=0).reshape(-1, width)
    gathered = call(
        gather_body,
        [shape(triples, width, dtype=BF)] * 2
        + [shape(width, triples, dtype=BF)] * 2
        + [shape(triples, width)]
        + [shape(triples, width, dtype=BF)] * 2,
        [pltpu.VMEM((heads.shape[0], 2 * width), BF), pltpu.VMEM((tails.shape[0], 2 * width), BF)],
        (cols, heads, tails),
    )
    (hv_hi, hv_lo, hvt_hi, hvt_lo, tv, n_hi, n_lo), own = lax.optimization_barrier((gathered, own))
    other = lax.ppermute(own, "c", SWAP)
    partial = call(
        functools.partial(query_body, 0), shape(triples, width), [], (core, cols, hv_hi, hv_lo, own), smem=1
    )
    f_hi, f_lo, d_hl = call(
        factor_body,
        [shape(triples, width, dtype=BF)] * 2 + [shape(2 * triples, 2 * width, dtype=BF)],
        [pltpu.VMEM((triples, width), F32)],
        (core, cols, hv_hi, hv_lo, tv, n_hi, n_lo, partial, other),
        smem=1,
    )

    tail_mine, tail_theirs = call(
        tail_body, [shape(tails.shape[0] // 2, width)] * 2, [], (core, rows, d_hl), smem=1
    )
    tail_came = lax.ppermute(tail_theirs, "c", SWAP)
    f_hi, tail_mine = lax.optimization_barrier((f_hi, tail_mine))

    def rel_part(half):
        args = (core, rows, hvt_hi, hvt_lo, f_hi, f_lo)
        return call(functools.partial(rel_body, half), shape(*own.shape), [], args, smem=1)

    rel_other = rel_part(1)
    rel_came = lax.ppermute(rel_other, "c", SWAP)
    f_hi, tail_sum, rel_other = lax.optimization_barrier((f_hi, tail_mine + tail_came, rel_other))
    tail_share = exchange_sum(tail_sum, HEAD_CHIPS)

    rel_own = rel_part(0)
    f_hi, rel_sum = lax.optimization_barrier((f_hi, rel_own + rel_came))
    rel_share = exchange_sum(rel_sum, CHIPS)

    head_grad = call(
        head_body,
        shape(*heads.shape),
        [pltpu.VMEM((triples, width), F32), pltpu.VMEM((triples, 2 * width), BF)],
        (core, cols, rows, f_hi, f_lo, own, other),
        smem=1,
    )
    head_share = permute_sum(head_grad, TAIL)
    return (head_share[None], tail_share[None], rel_share)


def solution(mesh):
    fine = Mesh(mesh.devices.reshape(4, 2, 2, 2, 4), ("y", "zh", "c", "zl", "x"))
    placed = (
        P(HEAD, None, None),
        P(TAIL, None, None),
        P(HEAD + TAIL, None),
        P(HEAD, TAIL, None, None, None),
        P(HEAD, TAIL, None, None, None),
        P(HEAD, TAIL, None, None, None),
        P(HEAD, TAIL, None, None, None),
    )
    return jax.shard_map(
        per_device,
        mesh=fine,
        in_specs=placed,
        out_specs=(P(HEAD, TAIL, None), P(TAIL, HEAD, None), P(HEAD + TAIL, None)),
        check_vma=False,
    )
```

```python
import functools

import jax
import jax.numpy as jnp
from jax import lax
from jax.experimental import pallas as pl
from jax.experimental.pallas import tpu as pltpu
from jax.sharding import Mesh, PartitionSpec as P

BF = jnp.bfloat16
F32 = jnp.float32
CHIPS = ("y", "zh", "zl", "x")
HEAD = ("y", "zh", "c")
HEAD_CHIPS = ("y", "zh")
TAIL = ("zl", "x")
SWAP = [(0, 1), (1, 0)]
NN = (((1,), (0,)), ((), ()))
NT = (((1,), (1,)), ((), ()))
TN = (((0,), (0,)), ((), ()))


def split(value):
    high = value.astype(BF)
    return high, (value - high.astype(F32)).astype(BF)


def dot(a, b, dims=NN):
    return lax.dot_general(a, b, dims, preferred_element_type=F32)


def dot3(a, b, dims=NN):
    return dot(a[0], b[0], dims) + dot(a[0], b[1], dims) + dot(a[1], b[0], dims)


def ones_where(mask):
    return jnp.where(mask, 1.0, 0.0).astype(BF)


def call(body, out_shape, scratch, args, smem=0, hbm=0, vmem=20):
    spaces = [pltpu.SMEM] * smem + [pltpu.HBM] * hbm
    spaces += [pltpu.VMEM] * (len(args) - smem - hbm)
    if hbm:
        fetched = [pltpu.with_memory_space_constraint(a, pltpu.HBM) for a in args[smem : smem + hbm]]
        args = tuple(args[:smem]) + tuple(fetched) + tuple(args[smem + hbm :])
        scratch = [pltpu.SemaphoreType.DMA((hbm,))] + [pltpu.VMEM(a.shape, a.dtype) for a in fetched] + scratch
    return pl.pallas_call(
        body,
        out_shape=out_shape,
        in_specs=[pl.BlockSpec(memory_space=space) for space in spaces],
        out_specs=jax.tree.map(lambda _: pl.BlockSpec(memory_space=pltpu.VMEM), out_shape),
        scratch_shapes=scratch,
        compiler_params=pltpu.CompilerParams(vmem_limit_bytes=vmem << 20),
    )(*args)


def fetch(sources, places, sems):
    copies = [pltpu.make_async_copy(a, b, sems.at[i]) for i, (a, b) in enumerate(zip(sources, places))]
    for copy in copies:
        copy.start()
    return copies


def slot_of(rel, core):
    return (rel >> 1) + jnp.where((rel & 1) == core, 0, 8)


def gather_body(
    core_ref, cols, rows_ref, head, tail,
    hv_hi, hv_lo, hvt_hi, hvt_lo, tv, n_hi, n_lo, rank_col, meta, head_hl, tail_hl, head_col,
):
    core = core_ref[0]
    width = head.shape[1]
    triples = cols.shape[0]
    high, low = split(head[...])
    head_hl[:, :width] = high
    head_hl[:, width:] = low
    high, low = split(tail[...])
    tail_hl[:, :width] = high
    tail_hl[:, width:] = low
    step = 256
    chunks = triples // step
    lanes = lax.broadcasted_iota(jnp.int32, (1, triples), 1)
    sublanes = lax.broadcasted_iota(jnp.int32, (step, 1), 0)
    key_row = slot_of(rows_ref[2:3, :], core) * triples + lanes
    rank_row = jnp.zeros((1, triples), F32)
    for i in range(chunks):
        part = slice(i * step, (i + 1) * step)
        key_col = slot_of(cols[part, 2:3], core) * triples + sublanes + i * step
        rank_row += jnp.sum(jnp.where(key_col < key_row, 1.0, 0.0), axis=0, keepdims=True)
        rank = jnp.sum(jnp.where(key_row < key_col, 1.0, 0.0), axis=1, keepdims=True)
        rank_col[part, :] = rank.astype(jnp.int32)
    rank_row = rank_row.astype(jnp.int32)
    head_row = jnp.zeros((1, triples), F32)
    head_ids = rows_ref[0:1, :].astype(F32)
    for i in range(chunks):
        part = slice(i * step, (i + 1) * step)
        here = rank_col[part, :] == lanes
        head_row += jnp.sum(jnp.where(here, cols[part, 0:1].astype(F32), 0.0), axis=0, keepdims=True)
        here = sublanes + i * step == rank_row
        head_col[part, :] = jnp.sum(jnp.where(here, head_ids, 0.0), axis=1, keepdims=True).astype(jnp.int32)
    meta[0:1, :] = rank_row
    meta[1:2, :] = head_row.astype(jnp.int32)

    def chunk(i, carry):
        rows = pl.ds(pl.multiple_of(i * step, step), step)
        part = cols[rows, :]

        def pick(index, table):
            ids = lax.broadcasted_iota(jnp.int32, (step, table.shape[0]), 1)
            return dot(ones_where(index == ids), table[...])

        both = pick(head_col[rows, :], head_hl)
        high, low = both[:, :width], both[:, width:]
        hv_hi[rows, :] = high.astype(BF)
        hv_lo[rows, :] = low.astype(BF)
        hvt_hi[:, rows] = jnp.transpose(high).astype(BF)
        hvt_lo[:, rows] = jnp.transpose(low).astype(BF)
        both = pick(part[:, 1:2], tail_hl)
        tv[rows, :] = both[:, :width] + both[:, width:]
        both = pick(part[:, 3:4], tail_hl)
        n_hi[rows, :] = both[:, :width].astype(BF)
        n_lo[rows, :] = both[:, width:].astype(BF)
        return carry

    lax.fori_loop(0, chunks, chunk, 0)


def split_rels(own, other, r_hi, r_lo, copies=None):
    count = own.shape[0]
    for half, mats in enumerate((own, other)):
        if copies:
            copies[half].wait()
        high, low = split(mats[...])
        r_hi[half * count : (half + 1) * count, :] = high
        r_lo[half * count : (half + 1) * count, :] = low


def visits(segs, tile, total, one, low=0, high=None):
    group = 4

    def some(g, carry):
        for k in range(group):
            v = g * group + k
            first = segs[0, v]
            one(pl.multiple_of(jnp.minimum(first // tile, total // tile - 1) * tile, tile), first, segs[1, v], segs[2, v])
        return carry

    lax.fori_loop(low, segs.shape[1] // group if high is None else high, some, 0)


def by_relation(segs, a_hi, a_lo, r_hi, r_lo, out, dims):
    width = r_hi.shape[1]
    tile = 128
    out[...] = jnp.zeros_like(out)

    def one(start, first, last, slot):
        rows = pl.ds(start, tile)
        place = start + lax.broadcasted_iota(jnp.int32, (tile, 1), 0)
        mask = ones_where((place >= first) & (place < last))
        high = a_hi[rows, :] * mask
        both = jnp.concatenate([high, a_lo[rows, :] * mask], axis=0)
        mat = pl.ds(pl.multiple_of(slot * width, width), width)
        main = dot(both, r_hi[mat, :], dims)
        out[rows, :] += main[:tile] + main[tile:] + dot(high, r_lo[mat, :], dims)

    visits(segs, tile, out.shape[0], one)


def factor_body(
    segs, own_at, other_at, hv_hi_at, hv_lo_at, rank_at, tv_at, n_hi_at, n_lo_at, meta,
    f_hi, f_lo, d_hl, sems, own, other, hv_hi, hv_lo, rank_col, tv, n_hi, n_lo, r_hi, r_lo, query, pair, f_hl,
):
    width = own.shape[1]
    triples = tv.shape[0]
    batch = triples // 2
    copies = fetch(
        (own_at, other_at, hv_hi_at, hv_lo_at, rank_at, tv_at, n_hi_at, n_lo_at),
        (own, other, hv_hi, hv_lo, rank_col, tv, n_hi, n_lo),
        sems,
    )
    split_rels(own, other, r_hi, r_lo, copies)
    for copy in copies[2:]:
        copy.wait()
    by_relation(segs, hv_hi, hv_lo, r_hi, r_lo, query, NN)
    high, low = split(query[...])
    pair[:, :width] = high
    pair[:, width:] = low
    for s in range(2):
        rows = slice(s * batch, (s + 1) * batch)
        ids = lax.broadcasted_iota(jnp.int32, (batch, triples), 1)
        both = dot(ones_where(rank_col[rows, :] == ids), pair[...])
        high, low = both[:, :width], both[:, width:]
        q = high + low
        q2 = (high.astype(BF), low.astype(BF))
        n2 = (n_hi[rows, :], n_lo[rows, :])
        weights = split(jax.nn.sigmoid(dot3(q2, n2, NT)) * (1.0 / batch))
        vec = tv[rows, :]
        coef = -jax.nn.sigmoid(-jnp.sum(q * vec, axis=1, keepdims=True))
        high, low = split(coef * vec + dot3(weights, n2))
        f_hl[rows, :width] = high
        f_hl[rows, width:] = low
        high, low = split(coef * q)
        d_hl[rows, :width] = high
        d_hl[rows, width:] = low
        high, low = split(dot3(weights, q2, TN))
        below = slice(triples + s * batch, triples + (s + 1) * batch)
        d_hl[below, :width] = high
        d_hl[below, width:] = low
    rank_row = meta[0:1, :]
    for s in range(2):
        rows = slice(s * batch, (s + 1) * batch)
        ids = lax.broadcasted_iota(jnp.int32, (batch, triples), 0) + s * batch
        both = dot(ones_where(ids == rank_row), f_hl[...])
        f_hi[rows, :] = both[:, :width].astype(BF)
        f_lo[rows, :] = both[:, width:].astype(BF)


def rel_body(half, segs, bounds, hvt_hi, hvt_lo, f_hi, f_lo, out):
    width = f_hi.shape[1]
    tile = 256
    count = out.shape[0] // width
    out[...] = jnp.zeros_like(out)

    def one(start, first, last, slot):
        part = pl.ds(start, tile)
        mine = (slot < count) if half == 0 else (slot >= count)
        last = jnp.where(mine, last, first)
        slot = jnp.minimum(slot, count - 1) if half == 0 else jnp.maximum(slot - count, 0)
        place = start + lax.broadcasted_iota(jnp.int32, (1, tile), 1)
        mask = ones_where((place >= first) & (place < last))
        high = hvt_hi[:, part] * mask
        both = jnp.concatenate([high, hvt_lo[:, part] * mask], axis=0)
        main = dot(both, f_hi[part, :])
        rows = pl.ds(pl.multiple_of(slot * width, width), width)
        out[rows, :] += main[:width] + main[width:] + dot(high, f_lo[part, :])

    visits(segs, tile, f_hi.shape[0], one, bounds[half, 0], bounds[half, 1])


def own_body(
    by_column, bounds, by_row, hvt_hi_at, hvt_lo_at, f_hi_at, f_lo_at, own_at, other_at, meta,
    rel_own, head_grad, sems, hvt_hi, hvt_lo, f_hi, f_lo, own, other, r_hi, r_lo, through, th_hl,
):
    copies = fetch(
        (hvt_hi_at, hvt_lo_at, f_hi_at, f_lo_at, own_at, other_at),
        (hvt_hi, hvt_lo, f_hi, f_lo, own, other),
        sems,
    )
    for copy in copies[:4]:
        copy.wait()
    rel_body(0, by_column, bounds, hvt_hi, hvt_lo, f_hi, f_lo, rel_own)
    split_rels(own, other, r_hi, r_lo, copies[4:])
    head_part(by_row, meta, f_hi, f_lo, head_grad, r_hi, r_lo, through, th_hl)


def tail_body(half, core_ref, rows_ref, d_hl, out):
    core = core_ref[0]
    width = out.shape[1]
    ids = jnp.concatenate([rows_ref[1:2, :], rows_ref[3:4, :]], axis=1)
    step = 512
    block = 128
    parity = core if half == 0 else 1 - core

    def chunk(i, carry):
        place = i * step + lax.broadcasted_iota(jnp.int32, (step, ids.shape[1]), 0)
        row = (place >> 7) * (2 * block) + parity * block + (place & (block - 1))
        both = dot(ones_where(row == ids), d_hl[...])
        rows = pl.ds(pl.multiple_of(i * step, step), step)
        out[rows, :] = both[:, :width] + both[:, width:]
        return carry

    lax.fori_loop(0, out.shape[0] // step, chunk, 0)


def head_part(segs, meta, f_hi, f_lo, out, r_hi, r_lo, through, th_hl):
    width = out.shape[1]
    by_relation(segs, f_hi, f_lo, r_hi, r_lo, through, NT)
    high, low = split(through[...])
    th_hl[:, :width] = high
    th_hl[:, width:] = low
    ids = meta[1:2, :]
    place = lax.broadcasted_iota(jnp.int32, (out.shape[0], ids.shape[1]), 0)
    both = dot(ones_where(place == ids), th_hl[...])
    out[...] = both[:, :width] + both[:, width:]


def shape(*dims, dtype=F32):
    return jax.ShapeDtypeStruct(dims, dtype)


def after(value, earlier):
    return lax.optimization_barrier((value, earlier))[0]


def exchange_sum(value, axes):
    devices = lax.axis_size(axes)
    pieces = value.reshape(devices, value.shape[0] // devices, value.shape[1])
    return jnp.sum(lax.all_to_all(pieces, axes, split_axis=0, concat_axis=0), axis=0)


def segments(starts, tile, total):
    edges = jnp.concatenate([jnp.arange(0, total, tile, dtype=jnp.int32), starts[1:]])
    count = edges.shape[0]
    place = jnp.arange(count)
    ahead = (edges[None, :] < edges[:, None]) | (
        (edges[None, :] == edges[:, None]) & (place[None, :] < place[:, None])
    )
    rank = jnp.sum(ahead.astype(jnp.int32), axis=1)
    padded = -(-count // 4) * 4
    at = jnp.arange(padded + 1)
    ordered = jnp.sum(jnp.where(rank[None, :] == at[:, None], edges[None, :], 0), axis=1)
    ordered = jnp.where(at < count, ordered, total)
    first = ordered[:padded]
    slot = jnp.sum((starts[None, 1:] <= first[:, None]).astype(jnp.int32), axis=1)
    return jnp.stack([first, ordered[1:], slot]).astype(jnp.int32)


def permute_sum(value, axis):
    devices = lax.axis_size(axis)
    me = lax.axis_index(axis)
    total = lax.dynamic_index_in_dim(value, me, 0, keepdims=False)
    for k in range(1, devices):
        piece = lax.dynamic_index_in_dim(value, me ^ k, 0, keepdims=False)
        total += lax.ppermute(piece, axis, [(i, i ^ k) for i in range(devices)])
    return total


def per_device(head_emb, tail_emb, relations, head_index, tail_index, rel_index, neg_index):
    width = relations.shape[1]
    heads = head_emb[0]
    tails = tail_emb[0]
    batch = head_index.shape[4]
    triples = 2 * batch
    index = jnp.stack([a[0, 0, :, 0] for a in (head_index, tail_index, rel_index, neg_index)], axis=1)
    behind = lax.axis_size(TAIL)
    next_index = lax.ppermute(index[1], TAIL, [(i, (i - 1) % behind) for i in range(behind)])
    core = lax.axis_index("c").astype(jnp.int32).reshape(1)

    chips = lax.axis_size(CHIPS)
    spread = jnp.broadcast_to(relations[None], (chips,) + relations.shape)
    spread, next_index = lax.optimization_barrier((spread, next_index))
    rows = jnp.concatenate([index[0], next_index], axis=1)
    cols = jnp.transpose(rows)
    own = lax.all_to_all(spread, CHIPS, split_axis=0, concat_axis=0).reshape(-1, width)
    slots = slot_of(rows[2], core)
    rel_count = chips * relations.shape[0] * 2 // width
    starts = jnp.sum((slots[None, :] < jnp.arange(rel_count)[:, None]).astype(jnp.int32), axis=1)
    by_row = segments(starts, 128, triples)
    by_column = segments(starts, 256, triples)
    middle = jnp.sum((by_column[0] < starts[rel_count // 2]).astype(jnp.int32))
    groups = jnp.full_like(middle, by_column.shape[1] // 4)
    zero = jnp.zeros_like(middle)
    bounds = jnp.stack([jnp.stack([zero, (middle + 3) // 4]), jnp.stack([middle // 4, groups])])
    wide = shape(triples, width, dtype=BF)
    high = shape(width, triples, dtype=BF)
    gathered = call(
        gather_body,
        [wide, wide, high, high, shape(triples, width), wide, wide]
        + [shape(triples, 1, dtype=jnp.int32), shape(2, triples, dtype=jnp.int32)],
        [
            pltpu.VMEM((heads.shape[0], 2 * width), BF),
            pltpu.VMEM((tails.shape[0], 2 * width), BF),
            pltpu.VMEM((triples, 1), jnp.int32),
        ],
        (core, cols, rows, heads, tails),
        smem=1,
    )
    hv_hi, hv_lo, hvt_hi, hvt_lo, tv, n_hi, n_lo, rank_col, meta = gathered
    meta, own, by_row, by_column, bounds = lax.optimization_barrier((meta, own, by_row, by_column, bounds))
    other = lax.ppermute(own, "c", SWAP)
    rel_scratch = [pltpu.VMEM((2 * own.shape[0], width), BF)] * 2
    f_hi, f_lo, d_hl = call(
        factor_body,
        [wide, wide, shape(2 * triples, 2 * width, dtype=BF)],
        rel_scratch + [pltpu.VMEM((triples, width), F32)] + [pltpu.VMEM((triples, 2 * width), BF)] * 2,
        (by_row, own, other, hv_hi, hv_lo, rank_col, tv, n_hi, n_lo, meta),
        smem=1,
        hbm=8,
        vmem=32,
    )

    def tail_part(half, core):
        out = shape(tails.shape[0] // 2, width)
        return call(functools.partial(tail_body, half), out, [], (core, rows, d_hl), smem=1)

    tail_theirs = tail_part(1, core)
    tail_came = lax.ppermute(tail_theirs, "c", SWAP)
    tail_mine = tail_part(0, after(core, tail_theirs))
    tail_sum = tail_mine + tail_came
    bounds = after(bounds, tail_sum)
    tail_share = exchange_sum(tail_sum, HEAD_CHIPS)

    rel_other = call(
        functools.partial(rel_body, 1),
        shape(*own.shape),
        [],
        (by_column, bounds, hvt_hi, hvt_lo, f_hi, f_lo),
        smem=2,
    )
    rel_came = lax.ppermute(rel_other, "c", SWAP)
    bounds = after(bounds, rel_other)
    rel_own, head_grad = call(
        own_body,
        [shape(*own.shape), shape(*heads.shape)],
        rel_scratch + [pltpu.VMEM((triples, width), F32), pltpu.VMEM((triples, 2 * width), BF)],
        (by_column, bounds, by_row, hvt_hi, hvt_lo, f_hi, f_lo, own, other, meta),
        smem=3,
        hbm=6,
        vmem=32,
    )
    rel_share = exchange_sum(rel_own + rel_came, CHIPS)
    pieces = head_grad.reshape(lax.axis_size("zl"), lax.axis_size("x"), -1, width)
    pieces = permute_sum(jnp.swapaxes(pieces, 0, 1), "x")
    head_share = permute_sum(after(pieces, tail_share), "zl")
    return (head_share[None], tail_share[None], rel_share)


def solution(mesh):
    fine = Mesh(mesh.devices.reshape(4, 2, 2, 2, 4), ("y", "zh", "c", "zl", "x"))
    placed = (
        P(HEAD, None, None),
        P(TAIL, None, None),
        P(HEAD + TAIL, None),
        P(HEAD, TAIL, None, None, None),
        P(HEAD, TAIL, None, None, None),
        P(HEAD, TAIL, None, None, None),
        P(HEAD, TAIL, None, None, None),
    )
    return jax.shard_map(
        per_device,
        mesh=fine,
        in_specs=placed,
        out_specs=(P(HEAD, TAIL, None), P(TAIL, HEAD, None), P(HEAD + TAIL, None)),
        check_vma=False,
    )
```

```python
import functools

import jax
import jax.numpy as jnp
from jax import lax
from jax.experimental import pallas as pl
from jax.experimental.pallas import tpu as pltpu
from jax.sharding import Mesh, PartitionSpec as P

BF = jnp.bfloat16
F32 = jnp.float32
CHIPS = ("y", "zh", "zl", "x")
HEAD = ("y", "zh", "c")
HEAD_CHIPS = ("y", "zh")
TAIL = ("zl", "x")
SWAP = [(0, 1), (1, 0)]
NN = (((1,), (0,)), ((), ()))
NT = (((1,), (1,)), ((), ()))
TN = (((0,), (0,)), ((), ()))


def split(value):
    high = value.astype(BF)
    return high, (value - high.astype(F32)).astype(BF)


def dot(a, b, dims=NN):
    return lax.dot_general(a, b, dims, preferred_element_type=F32)


def dot3(a, b, dims=NN):
    return dot(a[0], b[0], dims) + dot(a[0], b[1], dims) + dot(a[1], b[0], dims)


def ones_where(mask):
    return jnp.where(mask, 1.0, 0.0).astype(BF)


def call(body, out_shape, scratch, args, smem=0, hbm=0, keep=None, vmem=20):
    spaces = [pltpu.SMEM] * smem + [pltpu.HBM] * hbm
    spaces += [pltpu.VMEM] * (len(args) - smem - hbm)
    if hbm:
        fetched = [pltpu.with_memory_space_constraint(a, pltpu.HBM) for a in args[smem : smem + hbm]]
        args = tuple(args[:smem]) + tuple(fetched) + tuple(args[smem + hbm :])
        scratch = [pltpu.SemaphoreType.DMA((hbm,))] + [pltpu.VMEM(a.shape, a.dtype) for a in fetched[:keep]] + scratch
    return pl.pallas_call(
        body,
        out_shape=out_shape,
        in_specs=[pl.BlockSpec(memory_space=space) for space in spaces],
        out_specs=jax.tree.map(lambda _: pl.BlockSpec(memory_space=pltpu.VMEM), out_shape),
        scratch_shapes=scratch,
        compiler_params=pltpu.CompilerParams(vmem_limit_bytes=vmem << 20),
    )(*args)


def fetch(sources, places, sems):
    copies = [pltpu.make_async_copy(a, b, sems.at[i]) for i, (a, b) in enumerate(zip(sources, places))]
    for copy in copies:
        copy.start()
    return copies


def slot_of(rel, core):
    return (rel >> 1) + jnp.where((rel & 1) == core, 0, 8)


def gather_body(
    core_ref, cols, rows_ref, head, tail,
    hv_hi, hv_lo, hvt_hi, hvt_lo, tv, n_hi, n_lo, rank_col, meta, head_hl, tail_hl, head_col,
):
    core = core_ref[0]
    width = head.shape[1]
    triples = cols.shape[0]
    high, low = split(head[...])
    head_hl[:, :width] = high
    head_hl[:, width:] = low
    high, low = split(tail[...])
    tail_hl[:, :width] = high
    tail_hl[:, width:] = low
    step = 256
    chunks = triples // step
    lanes = lax.broadcasted_iota(jnp.int32, (1, triples), 1)
    sublanes = lax.broadcasted_iota(jnp.int32, (step, 1), 0)
    key_row = slot_of(rows_ref[2:3, :], core) * triples + lanes
    rank_row = jnp.zeros((1, triples), F32)
    for i in range(chunks):
        part = slice(i * step, (i + 1) * step)
        key_col = slot_of(cols[part, 2:3], core) * triples + sublanes + i * step
        rank_row += jnp.sum(jnp.where(key_col < key_row, 1.0, 0.0), axis=0, keepdims=True)
        rank = jnp.sum(jnp.where(key_row < key_col, 1.0, 0.0), axis=1, keepdims=True)
        rank_col[part, :] = rank.astype(jnp.int32)
    rank_row = rank_row.astype(jnp.int32)
    head_row = jnp.zeros((1, triples), F32)
    head_ids = rows_ref[0:1, :].astype(F32)
    for i in range(chunks):
        part = slice(i * step, (i + 1) * step)
        here = rank_col[part, :] == lanes
        head_row += jnp.sum(jnp.where(here, cols[part, 0:1].astype(F32), 0.0), axis=0, keepdims=True)
        here = sublanes + i * step == rank_row
        head_col[part, :] = jnp.sum(jnp.where(here, head_ids, 0.0), axis=1, keepdims=True).astype(jnp.int32)
    meta[0:1, :] = rank_row
    meta[1:2, :] = head_row.astype(jnp.int32)

    def chunk(i, carry):
        rows = pl.ds(pl.multiple_of(i * step, step), step)
        part = cols[rows, :]

        def pick(index, table):
            ids = lax.broadcasted_iota(jnp.int32, (step, table.shape[0]), 1)
            return dot(ones_where(index == ids), table[...])

        both = pick(head_col[rows, :], head_hl)
        high, low = both[:, :width], both[:, width:]
        hv_hi[rows, :] = high.astype(BF)
        hv_lo[rows, :] = low.astype(BF)
        hvt_hi[:, rows] = jnp.transpose(high).astype(BF)
        hvt_lo[:, rows] = jnp.transpose(low).astype(BF)
        both = pick(part[:, 1:2], tail_hl)
        tv[rows, :] = both[:, :width] + both[:, width:]
        both = pick(part[:, 3:4], tail_hl)
        n_hi[rows, :] = both[:, :width].astype(BF)
        n_lo[rows, :] = both[:, width:].astype(BF)
        return carry

    lax.fori_loop(0, chunks, chunk, 0)


def split_rels(halves, r_hi, r_lo, copies=None):
    for half, mats in enumerate(halves):
        count = mats.shape[0]
        if copies:
            copies[half].wait()
        high, low = split(mats[...])
        r_hi[half * count : (half + 1) * count, :] = high
        r_lo[half * count : (half + 1) * count, :] = low


def keep_half(half, count, first, last, slot):
    if half is None:
        return last, slot
    if half == 0:
        return jnp.where(slot < count, last, first), jnp.minimum(slot, count - 1)
    return jnp.where(slot >= count, last, first), jnp.maximum(slot - count, 0)


def visits(segs, tile, total, one, low=0, high=None):
    group = 4

    def some(g, carry):
        for k in range(group):
            v = g * group + k
            first = segs[0, v]
            one(pl.multiple_of(jnp.minimum(first // tile, total // tile - 1) * tile, tile), first, segs[1, v], segs[2, v])
        return carry

    lax.fori_loop(low, segs.shape[1] // group if high is None else high, some, 0)


def by_relation(segs, a_hi, a_lo, r_hi, r_lo, out, dims, half=None, low=0, high=None):
    width = r_hi.shape[1]
    tile = 128

    def one(start, first, last, slot):
        last, slot = keep_half(half, r_hi.shape[0] // width, first, last, slot)
        rows = pl.ds(start, tile)
        place = start + lax.broadcasted_iota(jnp.int32, (tile, 1), 0)
        mask = ones_where((place >= first) & (place < last))
        top = a_hi[rows, :] * mask
        both = jnp.concatenate([top, a_lo[rows, :] * mask], axis=0)
        mat = pl.ds(pl.multiple_of(slot * width, width), width)
        main = dot(both, r_hi[mat, :], dims)
        out[rows, :] += main[:tile] + main[tile:] + dot(top, r_lo[mat, :], dims)

    visits(segs, tile, out.shape[0], one, low, high)


def query_body(
    segs, bounds, own_at, hv_hi_at, hv_lo_at, tv_at, n_hi_at, n_lo_at, rank_at,
    query, hv_hi, hv_lo, tv, n_hi, n_lo, rank_col, sems, own, r_hi, r_lo,
):
    sources = (own_at, hv_hi_at, hv_lo_at, tv_at, n_hi_at, n_lo_at, rank_at)
    copies = fetch(sources, (own, hv_hi, hv_lo, tv, n_hi, n_lo, rank_col), sems)
    query[...] = jnp.zeros_like(query)
    split_rels((own,), r_hi, r_lo, copies)
    copies[1].wait()
    copies[2].wait()
    by_relation(segs, hv_hi, hv_lo, r_hi, r_lo, query, NN, 0, bounds[0, 0], bounds[0, 1])
    for copy in copies[3:]:
        copy.wait()


def factor_body(
    segs, bounds, partial, hv_hi, hv_lo, tv, n_hi, n_lo, rank_col, other, meta,
    f_hi, f_lo, d_hl, r_hi, r_lo, query, pair, f_hl,
):
    width = other.shape[1]
    triples = tv.shape[0]
    batch = triples // 2
    query[...] = partial[...]
    split_rels((other,), r_hi, r_lo)
    by_relation(segs, hv_hi, hv_lo, r_hi, r_lo, query, NN, 1, bounds[1, 0], bounds[1, 1])
    high, low = split(query[...])
    pair[:, :width] = high
    pair[:, width:] = low
    for s in range(2):
        rows = slice(s * batch, (s + 1) * batch)
        ids = lax.broadcasted_iota(jnp.int32, (batch, triples), 1)
        both = dot(ones_where(rank_col[rows, :] == ids), pair[...])
        high, low = both[:, :width], both[:, width:]
        q = high + low
        q2 = (high.astype(BF), low.astype(BF))
        n2 = (n_hi[rows, :], n_lo[rows, :])
        weights = split(jax.nn.sigmoid(dot3(q2, n2, NT)) * (1.0 / batch))
        vec = tv[rows, :]
        coef = -jax.nn.sigmoid(-jnp.sum(q * vec, axis=1, keepdims=True))
        high, low = split(coef * vec + dot3(weights, n2))
        f_hl[rows, :width] = high
        f_hl[rows, width:] = low
        high, low = split(coef * q)
        d_hl[rows, :width] = high
        d_hl[rows, width:] = low
        high, low = split(dot3(weights, q2, TN))
        below = slice(triples + s * batch, triples + (s + 1) * batch)
        d_hl[below, :width] = high
        d_hl[below, width:] = low
    rank_row = meta[0:1, :]
    for s in range(2):
        rows = slice(s * batch, (s + 1) * batch)
        ids = lax.broadcasted_iota(jnp.int32, (batch, triples), 0) + s * batch
        both = dot(ones_where(ids == rank_row), f_hl[...])
        f_hi[rows, :] = both[:, :width].astype(BF)
        f_lo[rows, :] = both[:, width:].astype(BF)


def rel_body(half, segs, bounds, hvt_hi, hvt_lo, f_hi, f_lo, out):
    width = f_hi.shape[1]
    tile = 256
    count = out.shape[0] // width
    out[...] = jnp.zeros_like(out)

    def one(start, first, last, slot):
        part = pl.ds(start, tile)
        last, slot = keep_half(half, count, first, last, slot)
        place = start + lax.broadcasted_iota(jnp.int32, (1, tile), 1)
        mask = ones_where((place >= first) & (place < last))
        high = hvt_hi[:, part] * mask
        both = jnp.concatenate([high, hvt_lo[:, part] * mask], axis=0)
        main = dot(both, f_hi[part, :])
        rows = pl.ds(pl.multiple_of(slot * width, width), width)
        out[rows, :] += main[:width] + main[width:] + dot(high, f_lo[part, :])

    visits(segs, tile, f_hi.shape[0], one, bounds[half, 0], bounds[half, 1])


def head_body(
    segs, f_hi_at, f_lo_at, own_at, other_at, meta, head_grad, sems, f_hi, f_lo, own, other, r_hi, r_lo, through, th_hl
):
    copies = fetch((f_hi_at, f_lo_at, own_at, other_at), (f_hi, f_lo, own, other), sems)
    split_rels((own, other), r_hi, r_lo, copies[2:])
    for copy in copies[:2]:
        copy.wait()
    head_part(segs, meta, f_hi, f_lo, head_grad, r_hi, r_lo, through, th_hl)


def tail_body(half, core_ref, rows_ref, d_hl, out):
    core = core_ref[0]
    width = out.shape[1]
    ids = jnp.concatenate([rows_ref[1:2, :], rows_ref[3:4, :]], axis=1)
    step = 512
    block = 128
    parity = core if half == 0 else 1 - core

    def chunk(i, carry):
        place = i * step + lax.broadcasted_iota(jnp.int32, (step, ids.shape[1]), 0)
        row = (place >> 7) * (2 * block) + parity * block + (place & (block - 1))
        both = dot(ones_where(row == ids), d_hl[...])
        rows = pl.ds(pl.multiple_of(i * step, step), step)
        out[rows, :] = both[:, :width] + both[:, width:]
        return carry

    lax.fori_loop(0, out.shape[0] // step, chunk, 0)


def head_part(segs, meta, f_hi, f_lo, out, r_hi, r_lo, through, th_hl):
    width = out.shape[1]
    through[...] = jnp.zeros_like(through)
    by_relation(segs, f_hi, f_lo, r_hi, r_lo, through, NT)
    high, low = split(through[...])
    th_hl[:, :width] = high
    th_hl[:, width:] = low
    ids = meta[1:2, :]
    place = lax.broadcasted_iota(jnp.int32, (out.shape[0], ids.shape[1]), 0)
    both = dot(ones_where(place == ids), th_hl[...])
    out[...] = both[:, :width] + both[:, width:]


def shape(*dims, dtype=F32):
    return jax.ShapeDtypeStruct(dims, dtype)


def half_bounds(segs, starts):
    middle = jnp.sum((segs[0] < starts[starts.shape[0] // 2]).astype(jnp.int32))
    end = jnp.full_like(middle, segs.shape[1] // 4)
    return jnp.stack([jnp.stack([jnp.zeros_like(middle), (middle + 3) // 4]), jnp.stack([middle // 4, end])])


def after(value, earlier):
    return lax.optimization_barrier((value, earlier))[0]


def exchange(value, axes):
    devices = lax.axis_size(axes)
    pieces = value.reshape(devices, value.shape[0] // devices, value.shape[1])
    return lax.all_to_all(pieces, axes, split_axis=0, concat_axis=0)


def segments(starts, tile, total):
    edges = jnp.concatenate([jnp.arange(0, total, tile, dtype=jnp.int32), starts[1:]])
    count = edges.shape[0]
    place = jnp.arange(count)
    ahead = (edges[None, :] < edges[:, None]) | (
        (edges[None, :] == edges[:, None]) & (place[None, :] < place[:, None])
    )
    rank = jnp.sum(ahead.astype(jnp.int32), axis=1)
    padded = -(-count // 4) * 4
    at = jnp.arange(padded + 1)
    ordered = jnp.sum(jnp.where(rank[None, :] == at[:, None], edges[None, :], 0), axis=1)
    ordered = jnp.where(at < count, ordered, total)
    first = ordered[:padded]
    slot = jnp.sum((starts[None, 1:] <= first[:, None]).astype(jnp.int32), axis=1)
    return jnp.stack([first, ordered[1:], slot]).astype(jnp.int32)


def permute_sum(value, axis, behind=None):
    devices = lax.axis_size(axis)
    me = lax.axis_index(axis)
    total = lax.dynamic_index_in_dim(value, me, 0, keepdims=False)
    if behind is not None:
        total = after(total, behind)
    for k in range(1, devices):
        piece = lax.dynamic_index_in_dim(value, me ^ k, 0, keepdims=False)
        total += lax.ppermute(piece, axis, [(i, i ^ k) for i in range(devices)])
    return total


def per_device(head_emb, tail_emb, relations, head_index, tail_index, rel_index, neg_index):
    width = relations.shape[1]
    heads = head_emb[0]
    tails = tail_emb[0]
    batch = head_index.shape[4]
    triples = 2 * batch
    index = jnp.stack([a[0, 0, :, 0] for a in (head_index, tail_index, rel_index, neg_index)], axis=1)
    behind = lax.axis_size(TAIL)
    next_index = lax.ppermute(index[1], TAIL, [(i, (i - 1) % behind) for i in range(behind)])
    core = lax.axis_index("c").astype(jnp.int32).reshape(1)

    chips = lax.axis_size(CHIPS)
    spread = jnp.broadcast_to(relations[None], (chips,) + relations.shape)
    spread, next_index = lax.optimization_barrier((spread, next_index))
    rows = jnp.concatenate([index[0], next_index], axis=1)
    cols = jnp.transpose(rows)
    own = lax.all_to_all(spread, CHIPS, split_axis=0, concat_axis=0).reshape(-1, width)
    slots = slot_of(rows[2], core)
    rel_count = chips * relations.shape[0] * 2 // width
    starts = jnp.sum((slots[None, :] < jnp.arange(rel_count)[:, None]).astype(jnp.int32), axis=1)
    by_row = segments(starts, 128, triples)
    by_column = segments(starts, 256, triples)
    row_bounds = half_bounds(by_row, starts)
    bounds = half_bounds(by_column, starts)
    wide = shape(triples, width, dtype=BF)
    high = shape(width, triples, dtype=BF)
    gathered = call(
        gather_body,
        [wide, wide, high, high, shape(triples, width), wide, wide]
        + [shape(triples, 1, dtype=jnp.int32), shape(2, triples, dtype=jnp.int32)],
        [
            pltpu.VMEM((heads.shape[0], 2 * width), BF),
            pltpu.VMEM((tails.shape[0], 2 * width), BF),
            pltpu.VMEM((triples, 1), jnp.int32),
        ],
        (core, cols, rows, heads, tails),
        smem=1,
    )
    hv_hi, hv_lo, hvt_hi, hvt_lo, tv, n_hi, n_lo, rank_col, meta = gathered
    meta, own, by_row, row_bounds, by_column, bounds = lax.optimization_barrier(
        (meta, own, by_row, row_bounds, by_column, bounds)
    )
    other = lax.ppermute(own, "c", SWAP)
    half_scratch = [pltpu.VMEM(own.shape, BF)] * 2
    plain = shape(triples, width)
    ready = call(
        query_body,
        [plain, wide, wide, plain, wide, wide, shape(triples, 1, dtype=jnp.int32)],
        half_scratch,
        (by_row, row_bounds, own, hv_hi, hv_lo, tv, n_hi, n_lo, rank_col),
        smem=2,
        hbm=7,
        keep=1,
    )
    f_hi, f_lo, d_hl = call(
        factor_body,
        [wide, wide, shape(2 * triples, 2 * width, dtype=BF)],
        half_scratch + [pltpu.VMEM((triples, width), F32)] + [pltpu.VMEM((triples, 2 * width), BF)] * 2,
        (by_row, row_bounds, *ready, other, meta),
        smem=2,
    )

    def rel_part(half, bounds):
        out = shape(*own.shape)
        args = (by_column, bounds, hvt_hi, hvt_lo, f_hi, f_lo)
        return call(functools.partial(rel_body, half), out, [], args, smem=2)

    def tail_part(half, core):
        out = shape(tails.shape[0] // 2, width)
        return call(functools.partial(tail_body, half), out, [], (core, rows, d_hl), smem=1)

    rel_other = rel_part(1, bounds)
    rel_came = lax.ppermute(rel_other, "c", SWAP)
    rel_own = rel_part(0, after(bounds, rel_other))
    tail_theirs = tail_part(1, after(core, rel_own))
    tail_came = lax.ppermute(tail_theirs, "c", SWAP)
    rel_sum = rel_own + rel_came
    rel_pieces = exchange(rel_sum, CHIPS)

    tail_mine = tail_part(0, after(core, rel_sum))
    head_grad = call(
        head_body,
        shape(*heads.shape),
        [pltpu.VMEM((2 * own.shape[0], width), BF)] * 2
        + [pltpu.VMEM((triples, width), F32), pltpu.VMEM((triples, 2 * width), BF)],
        (after(by_row, tail_mine), f_hi, f_lo, own, other, meta),
        smem=1,
        hbm=4,
        vmem=32,
    )
    pieces = head_grad.reshape(lax.axis_size("zl"), lax.axis_size("x"), -1, width)
    pieces = permute_sum(jnp.swapaxes(pieces, 0, 1), "x")
    tail_sum = after(tail_mine + tail_came, (pieces, rel_pieces))
    tail_share = jnp.sum(exchange(tail_sum, HEAD_CHIPS), axis=0)
    rel_share = jnp.sum(rel_pieces, axis=0)
    head_share = permute_sum(pieces, "zl", rel_share)
    return (head_share[None], tail_share[None], rel_share)


def solution(mesh):
    fine = Mesh(mesh.devices.reshape(4, 2, 2, 2, 4), ("y", "zh", "c", "zl", "x"))
    placed = (
        P(HEAD, None, None),
        P(TAIL, None, None),
        P(HEAD + TAIL, None),
        P(HEAD, TAIL, None, None, None),
        P(HEAD, TAIL, None, None, None),
        P(HEAD, TAIL, None, None, None),
        P(HEAD, TAIL, None, None, None),
    )
    return jax.shard_map(
        per_device,
        mesh=fine,
        in_specs=placed,
        out_specs=(P(HEAD, TAIL, None), P(TAIL, HEAD, None), P(HEAD + TAIL, None)),
        check_vma=False,
    )
```

```python
import functools

import jax
import jax.numpy as jnp
from jax import lax
from jax.experimental import pallas as pl
from jax.experimental.pallas import tpu as pltpu
from jax.sharding import Mesh, PartitionSpec as P

BF = jnp.bfloat16
F32 = jnp.float32
CHIPS = ("x", "zl", "zh", "y")
OWNERS = ("y", "zh", "zl", "x")
HEAD = ("y", "zh", "c")
HEAD_CHIPS = ("y", "zh")
TAIL = ("zl", "x")
SWAP = [(0, 1), (1, 0)]
NN = (((1,), (0,)), ((), ()))
NT = (((1,), (1,)), ((), ()))
TN = (((0,), (0,)), ((), ()))


def split(value):
    high = value.astype(BF)
    return high, (value - high.astype(F32)).astype(BF)


def dot(a, b, dims=NN):
    return lax.dot_general(a, b, dims, preferred_element_type=F32)


def dot3(a, b, dims=NN):
    return dot(a[0], b[0], dims) + dot(a[0], b[1], dims) + dot(a[1], b[0], dims)


def ones_where(mask):
    return jnp.where(mask, 1.0, 0.0).astype(BF)


def call(body, out_shape, scratch, args, smem=0, hbm=0, keep=None, vmem=20):
    spaces = [pltpu.SMEM] * smem + [pltpu.HBM] * hbm
    spaces += [pltpu.VMEM] * (len(args) - smem - hbm)
    if hbm:
        fetched = [pltpu.with_memory_space_constraint(a, pltpu.HBM) for a in args[smem : smem + hbm]]
        args = tuple(args[:smem]) + tuple(fetched) + tuple(args[smem + hbm :])
        scratch = [pltpu.SemaphoreType.DMA((hbm,))] + [pltpu.VMEM(a.shape, a.dtype) for a in fetched[:keep]] + scratch
    return pl.pallas_call(
        body,
        out_shape=out_shape,
        in_specs=[pl.BlockSpec(memory_space=space) for space in spaces],
        out_specs=jax.tree.map(lambda _: pl.BlockSpec(memory_space=pltpu.VMEM), out_shape),
        scratch_shapes=scratch,
        compiler_params=pltpu.CompilerParams(vmem_limit_bytes=vmem << 20),
    )(*args)


def fetch(sources, places, sems):
    copies = [pltpu.make_async_copy(a, b, sems.at[i]) for i, (a, b) in enumerate(zip(sources, places))]
    for copy in copies:
        copy.start()
    return copies


def slot_of(rel, core):
    return (rel >> 1) + jnp.where((rel & 1) == core, 0, 8)


def gather_body(
    core_ref, cols, rows_ref, head, tail,
    hv_hi, hv_lo, hvt_hi, hvt_lo, tv, n_hi, n_lo, rank_col, meta, head_hl, tail_hl, head_col,
):
    core = core_ref[0]
    width = head.shape[1]
    triples = cols.shape[0]
    high, low = split(head[...])
    head_hl[:, :width] = high
    head_hl[:, width:] = low
    high, low = split(tail[...])
    tail_hl[:, :width] = high
    tail_hl[:, width:] = low
    step = 256
    chunks = triples // step
    lanes = lax.broadcasted_iota(jnp.int32, (1, triples), 1)
    sublanes = lax.broadcasted_iota(jnp.int32, (step, 1), 0)
    key_row = slot_of(rows_ref[2:3, :], core) * triples + lanes
    rank_row = jnp.zeros((1, triples), F32)
    for i in range(chunks):
        part = slice(i * step, (i + 1) * step)
        key_col = slot_of(cols[part, 2:3], core) * triples + sublanes + i * step
        rank_row += jnp.sum(jnp.where(key_col < key_row, 1.0, 0.0), axis=0, keepdims=True)
        rank = jnp.sum(jnp.where(key_row < key_col, 1.0, 0.0), axis=1, keepdims=True)
        rank_col[part, :] = rank.astype(jnp.int32)
    rank_row = rank_row.astype(jnp.int32)
    head_row = jnp.zeros((1, triples), F32)
    head_ids = rows_ref[0:1, :].astype(F32)
    for i in range(chunks):
        part = slice(i * step, (i + 1) * step)
        here = rank_col[part, :] == lanes
        head_row += jnp.sum(jnp.where(here, cols[part, 0:1].astype(F32), 0.0), axis=0, keepdims=True)
        here = sublanes + i * step == rank_row
        head_col[part, :] = jnp.sum(jnp.where(here, head_ids, 0.0), axis=1, keepdims=True).astype(jnp.int32)
    meta[0:1, :] = rank_row
    meta[1:2, :] = head_row.astype(jnp.int32)

    def chunk(i, carry):
        rows = pl.ds(pl.multiple_of(i * step, step), step)
        part = cols[rows, :]

        def pick(index, table):
            ids = lax.broadcasted_iota(jnp.int32, (step, table.shape[0]), 1)
            return dot(ones_where(index == ids), table[...])

        both = pick(head_col[rows, :], head_hl)
        high, low = both[:, :width], both[:, width:]
        hv_hi[rows, :] = high.astype(BF)
        hv_lo[rows, :] = low.astype(BF)
        hvt_hi[:, rows] = jnp.transpose(high).astype(BF)
        hvt_lo[:, rows] = jnp.transpose(low).astype(BF)
        both = pick(part[:, 1:2], tail_hl)
        tv[rows, :] = both[:, :width] + both[:, width:]
        both = pick(part[:, 3:4], tail_hl)
        n_hi[rows, :] = both[:, :width].astype(BF)
        n_lo[rows, :] = both[:, width:].astype(BF)
        return carry

    lax.fori_loop(0, chunks, chunk, 0)


def order_of(piece):
    return (piece % 4) * 2 + piece // 4


def slot_order(slot):
    return (slot & 1) * 4 + (slot >> 1)


def split_rels(halves, r_hi, r_lo, copies=None):
    for half, mats in enumerate(halves):
        chips, deep = mats.shape[:2]
        if copies:
            copies[half].wait()
        for slot in range(8):
            for piece in range(chips // 8):
                high, low = split(mats[order_of(piece) * 8 + slot_order(slot)])
                start = (half * chips + slot * (chips // 8) + piece) * deep
                r_hi[start : start + deep, :] = high
                r_lo[start : start + deep, :] = low


def keep_half(half, count, first, last, slot):
    if half is None:
        return last, slot
    if half == 0:
        return jnp.where(slot < count, last, first), jnp.minimum(slot, count - 1)
    return jnp.where(slot >= count, last, first), jnp.maximum(slot - count, 0)


def visits(segs, tile, total, one, low=0, high=None):
    group = 4

    def some(g, carry):
        for k in range(group):
            v = g * group + k
            first = segs[0, v]
            one(pl.multiple_of(jnp.minimum(first // tile, total // tile - 1) * tile, tile), first, segs[1, v], segs[2, v])
        return carry

    lax.fori_loop(low, segs.shape[1] // group if high is None else high, some, 0)


def by_relation(segs, a_hi, a_lo, r_hi, r_lo, out, dims, half=None, low=0, high=None):
    width = r_hi.shape[1]
    tile = 128

    def one(start, first, last, slot):
        last, slot = keep_half(half, r_hi.shape[0] // width, first, last, slot)
        rows = pl.ds(start, tile)
        place = start + lax.broadcasted_iota(jnp.int32, (tile, 1), 0)
        mask = ones_where((place >= first) & (place < last))
        top = a_hi[rows, :] * mask
        both = jnp.concatenate([top, a_lo[rows, :] * mask], axis=0)
        mat = pl.ds(pl.multiple_of(slot * width, width), width)
        main = dot(both, r_hi[mat, :], dims)
        out[rows, :] += main[:tile] + main[tile:] + dot(top, r_lo[mat, :], dims)

    visits(segs, tile, out.shape[0], one, low, high)


def query_body(
    segs, bounds, own_at, hv_hi_at, hv_lo_at, tv_at, n_hi_at, n_lo_at, rank_at,
    query, hv_hi, hv_lo, tv, n_hi, n_lo, rank_col, sems, own, r_hi, r_lo,
):
    sources = (own_at, hv_hi_at, hv_lo_at, tv_at, n_hi_at, n_lo_at, rank_at)
    copies = fetch(sources, (own, hv_hi, hv_lo, tv, n_hi, n_lo, rank_col), sems)
    query[...] = jnp.zeros_like(query)
    split_rels((own,), r_hi, r_lo, copies)
    copies[1].wait()
    copies[2].wait()
    by_relation(segs, hv_hi, hv_lo, r_hi, r_lo, query, NN, 0, bounds[0, 0], bounds[0, 1])
    for copy in copies[3:]:
        copy.wait()


def factor_body(
    segs, bounds, partial, hv_hi, hv_lo, tv, n_hi, n_lo, rank_col, other, meta,
    f_hi, f_lo, d_hl, r_hi, r_lo, query, pair, f_hl,
):
    width = other.shape[2]
    triples = tv.shape[0]
    batch = triples // 2
    query[...] = partial[...]
    split_rels((other,), r_hi, r_lo)
    by_relation(segs, hv_hi, hv_lo, r_hi, r_lo, query, NN, 1, bounds[1, 0], bounds[1, 1])
    high, low = split(query[...])
    pair[:, :width] = high
    pair[:, width:] = low
    for s in range(2):
        rows = slice(s * batch, (s + 1) * batch)
        ids = lax.broadcasted_iota(jnp.int32, (batch, triples), 1)
        both = dot(ones_where(rank_col[rows, :] == ids), pair[...])
        high, low = both[:, :width], both[:, width:]
        q = high + low
        q2 = (high.astype(BF), low.astype(BF))
        n2 = (n_hi[rows, :], n_lo[rows, :])
        weights = split(jax.nn.sigmoid(dot3(q2, n2, NT)) * (1.0 / batch))
        vec = tv[rows, :]
        coef = -jax.nn.sigmoid(-jnp.sum(q * vec, axis=1, keepdims=True))
        high, low = split(coef * vec + dot3(weights, n2))
        f_hl[rows, :width] = high
        f_hl[rows, width:] = low
        high, low = split(coef * q)
        d_hl[rows, :width] = high
        d_hl[rows, width:] = low
        high, low = split(dot3(weights, q2, TN))
        below = slice(triples + s * batch, triples + (s + 1) * batch)
        d_hl[below, :width] = high
        d_hl[below, width:] = low
    rank_row = meta[0:1, :]
    for s in range(2):
        rows = slice(s * batch, (s + 1) * batch)
        ids = lax.broadcasted_iota(jnp.int32, (batch, triples), 0) + s * batch
        both = dot(ones_where(ids == rank_row), f_hl[...])
        f_hi[rows, :] = both[:, :width].astype(BF)
        f_lo[rows, :] = both[:, width:].astype(BF)


def rel_body(half, segs, bounds, hvt_hi, hvt_lo, f_hi, f_lo, out):
    width = f_hi.shape[1]
    tile = 256
    chips, deep = out.shape[:2]
    pieces = width // deep
    count = chips // pieces
    out[...] = jnp.zeros_like(out)

    def one(start, first, last, slot):
        part = pl.ds(start, tile)
        last, slot = keep_half(half, count, first, last, slot)
        place = start + lax.broadcasted_iota(jnp.int32, (1, tile), 1)
        mask = ones_where((place >= first) & (place < last))
        high = hvt_hi[:, part] * mask
        both = jnp.concatenate([high, hvt_lo[:, part] * mask], axis=0)
        main = dot(both, f_hi[part, :])
        total = main[:width] + main[width:] + dot(high, f_lo[part, :])
        for piece in range(pieces):
            out[slot * pieces + piece] += total[piece * deep : (piece + 1) * deep]

    visits(segs, tile, f_hi.shape[0], one, bounds[half, 0], bounds[half, 1])


def head_body(
    segs, f_hi_at, f_lo_at, own_at, other_at, meta, head_grad, sems, f_hi, f_lo, own, other, r_hi, r_lo, through, th_hl
):
    copies = fetch((f_hi_at, f_lo_at, own_at, other_at), (f_hi, f_lo, own, other), sems)
    split_rels((own, other), r_hi, r_lo, copies[2:])
    for copy in copies[:2]:
        copy.wait()
    head_part(segs, meta, f_hi, f_lo, head_grad, r_hi, r_lo, through, th_hl)


def tail_body(half, core_ref, rows_ref, d_hl, out):
    core = core_ref[0]
    width = out.shape[1]
    ids = jnp.concatenate([rows_ref[1:2, :], rows_ref[3:4, :]], axis=1)
    step = 512
    block = 128
    parity = core if half == 0 else 1 - core

    def chunk(i, carry):
        place = i * step + lax.broadcasted_iota(jnp.int32, (step, ids.shape[1]), 0)
        row = (place >> 7) * (2 * block) + parity * block + (place & (block - 1))
        both = dot(ones_where(row == ids), d_hl[...])
        rows = pl.ds(pl.multiple_of(i * step, step), step)
        out[rows, :] = both[:, :width] + both[:, width:]
        return carry

    lax.fori_loop(0, out.shape[0] // step, chunk, 0)


def head_part(segs, meta, f_hi, f_lo, out, r_hi, r_lo, through, th_hl):
    width = out.shape[1]
    through[...] = jnp.zeros_like(through)
    by_relation(segs, f_hi, f_lo, r_hi, r_lo, through, NT)
    high, low = split(through[...])
    th_hl[:, :width] = high
    th_hl[:, width:] = low
    ids = meta[1:2, :]
    place = lax.broadcasted_iota(jnp.int32, (out.shape[0], ids.shape[1]), 0)
    both = dot(ones_where(place == ids), th_hl[...])
    out[...] = both[:, :width] + both[:, width:]


def shape(*dims, dtype=F32):
    return jax.ShapeDtypeStruct(dims, dtype)


def half_bounds(segs, starts):
    middle = jnp.sum((segs[0] < starts[starts.shape[0] // 2]).astype(jnp.int32))
    end = jnp.full_like(middle, segs.shape[1] // 4)
    return jnp.stack([jnp.stack([jnp.zeros_like(middle), (middle + 3) // 4]), jnp.stack([middle // 4, end])])


def after(value, earlier):
    return lax.optimization_barrier((value, earlier))[0]


def exchange(value, axes):
    pieces = value.reshape(lax.axis_size(axes), -1, value.shape[-1])
    return lax.all_to_all(pieces, axes, split_axis=0, concat_axis=0)


def segments(starts, tile, total):
    edges = jnp.concatenate([jnp.arange(0, total, tile, dtype=jnp.int32), starts[1:]])
    count = edges.shape[0]
    place = jnp.arange(count)
    ahead = (edges[None, :] < edges[:, None]) | (
        (edges[None, :] == edges[:, None]) & (place[None, :] < place[:, None])
    )
    rank = jnp.sum(ahead.astype(jnp.int32), axis=1)
    padded = -(-count // 4) * 4
    at = jnp.arange(padded + 1)
    ordered = jnp.sum(jnp.where(rank[None, :] == at[:, None], edges[None, :], 0), axis=1)
    ordered = jnp.where(at < count, ordered, total)
    first = ordered[:padded]
    slot = jnp.sum((starts[None, 1:] <= first[:, None]).astype(jnp.int32), axis=1)
    return jnp.stack([first, ordered[1:], slot]).astype(jnp.int32)


def permute_sum(value, axis, behind=None):
    devices = lax.axis_size(axis)
    me = lax.axis_index(axis)
    total = lax.dynamic_index_in_dim(value, me, 0, keepdims=False)
    if behind is not None:
        total = after(total, behind)
    for k in range(1, devices):
        piece = lax.dynamic_index_in_dim(value, me ^ k, 0, keepdims=False)
        total += lax.ppermute(piece, axis, [(i, i ^ k) for i in range(devices)])
    return total


def per_device(head_emb, tail_emb, relations, head_index, tail_index, rel_index, neg_index):
    width = relations.shape[1]
    heads = head_emb[0]
    tails = tail_emb[0]
    batch = head_index.shape[4]
    triples = 2 * batch
    index = jnp.stack([a[0, 0, :, 0] for a in (head_index, tail_index, rel_index, neg_index)], axis=1)
    behind = lax.axis_size(TAIL)
    next_index = lax.ppermute(index[1], TAIL, [(i, (i - 1) % behind) for i in range(behind)])
    core = lax.axis_index("c").astype(jnp.int32).reshape(1)

    chips = lax.axis_size(CHIPS)
    spread = jnp.broadcast_to(relations[None], (chips,) + relations.shape)
    spread, next_index = lax.optimization_barrier((spread, next_index))
    rows = jnp.concatenate([index[0], next_index], axis=1)
    cols = jnp.transpose(rows)
    own = lax.all_to_all(spread, CHIPS, split_axis=0, concat_axis=0)
    slots = slot_of(rows[2], core)
    rel_count = 2 * lax.axis_size(HEAD_CHIPS)
    starts = jnp.sum((slots[None, :] < jnp.arange(rel_count)[:, None]).astype(jnp.int32), axis=1)
    by_row = segments(starts, 128, triples)
    by_column = segments(starts, 256, triples)
    row_bounds = half_bounds(by_row, starts)
    bounds = half_bounds(by_column, starts)
    wide = shape(triples, width, dtype=BF)
    high = shape(width, triples, dtype=BF)
    gathered = call(
        gather_body,
        [wide, wide, high, high, shape(triples, width), wide, wide]
        + [shape(triples, 1, dtype=jnp.int32), shape(2, triples, dtype=jnp.int32)],
        [
            pltpu.VMEM((heads.shape[0], 2 * width), BF),
            pltpu.VMEM((tails.shape[0], 2 * width), BF),
            pltpu.VMEM((triples, 1), jnp.int32),
        ],
        (core, cols, rows, heads, tails),
        smem=1,
    )
    hv_hi, hv_lo, hvt_hi, hvt_lo, tv, n_hi, n_lo, rank_col, meta = gathered
    meta, own, by_row, row_bounds, by_column, bounds = lax.optimization_barrier(
        (meta, own, by_row, row_bounds, by_column, bounds)
    )
    other = lax.ppermute(own, "c", SWAP)
    half_rows = own.shape[0] * own.shape[1]
    half_scratch = [pltpu.VMEM((half_rows, width), BF)] * 2
    plain = shape(triples, width)
    ready = call(
        query_body,
        [plain, wide, wide, plain, wide, wide, shape(triples, 1, dtype=jnp.int32)],
        half_scratch,
        (by_row, row_bounds, own, hv_hi, hv_lo, tv, n_hi, n_lo, rank_col),
        smem=2,
        hbm=7,
        keep=1,
    )
    f_hi, f_lo, d_hl = call(
        factor_body,
        [wide, wide, shape(2 * triples, 2 * width, dtype=BF)],
        half_scratch + [pltpu.VMEM((triples, width), F32)] + [pltpu.VMEM((triples, 2 * width), BF)] * 2,
        (by_row, row_bounds, *ready, other, meta),
        smem=2,
    )

    def rel_part(half, bounds):
        out = shape(*own.shape)
        args = (by_column, bounds, hvt_hi, hvt_lo, f_hi, f_lo)
        return call(functools.partial(rel_body, half), out, [], args, smem=2)

    def tail_part(half, core):
        out = shape(tails.shape[0] // 2, width)
        return call(functools.partial(tail_body, half), out, [], (core, rows, d_hl), smem=1)

    rel_other = rel_part(1, bounds)
    rel_came = lax.ppermute(rel_other, "c", SWAP)
    rel_own = rel_part(0, after(bounds, rel_other))
    tail_theirs = tail_part(1, after(core, rel_own))
    tail_came = lax.ppermute(tail_theirs, "c", SWAP)
    rel_sum = rel_own + rel_came
    rel_pieces = exchange(rel_sum, OWNERS)

    tail_mine = tail_part(0, after(core, rel_sum))
    head_grad = call(
        head_body,
        shape(*heads.shape),
        [pltpu.VMEM((2 * half_rows, width), BF)] * 2
        + [pltpu.VMEM((triples, width), F32), pltpu.VMEM((triples, 2 * width), BF)],
        (after(by_row, tail_mine), f_hi, f_lo, own, other, meta),
        smem=1,
        hbm=4,
        vmem=32,
    )
    pieces = head_grad.reshape(lax.axis_size("zl"), lax.axis_size("x"), -1, width)
    pieces = permute_sum(jnp.swapaxes(pieces, 0, 1), "x")
    tail_sum = after(tail_mine + tail_came, (head_grad, rel_pieces))
    tail_share = jnp.sum(exchange(tail_sum, HEAD_CHIPS), axis=0)
    rel_share = jnp.sum(rel_pieces, axis=0)
    head_share = permute_sum(pieces, "zl", rel_share)
    return (head_share[None], tail_share[None], rel_share)


def solution(mesh):
    fine = Mesh(mesh.devices.reshape(4, 2, 2, 2, 4), ("y", "zh", "c", "zl", "x"))
    placed = (
        P(HEAD, None, None),
        P(TAIL, None, None),
        P(HEAD + TAIL, None),
        P(HEAD, TAIL, None, None, None),
        P(HEAD, TAIL, None, None, None),
        P(HEAD, TAIL, None, None, None),
        P(HEAD, TAIL, None, None, None),
    )
    return jax.shard_map(
        per_device,
        mesh=fine,
        in_specs=placed,
        out_specs=(P(HEAD, TAIL, None), P(TAIL, HEAD, None), P(HEAD + TAIL, None)),
        check_vma=False,
    )
```

```python
import functools

import jax
import jax.numpy as jnp
from jax import lax
from jax.experimental import pallas as pl
from jax.experimental.pallas import tpu as pltpu
from jax.sharding import Mesh, PartitionSpec as P

BF = jnp.bfloat16
F32 = jnp.float32
CHIPS = ("x", "zl", "zh", "y")
OWNERS = ("y", "zh", "zl", "x")
HEAD = ("y", "zh", "c")
HEAD_CHIPS = ("y", "zh")
TAIL = ("zl", "x")
SWAP = [(0, 1), (1, 0)]
NN = (((1,), (0,)), ((), ()))
NT = (((1,), (1,)), ((), ()))
TN = (((0,), (0,)), ((), ()))


def split(value):
    high = value.astype(BF)
    return high, (value - high.astype(F32)).astype(BF)


def dot(a, b, dims=NN):
    return lax.dot_general(a, b, dims, preferred_element_type=F32)


def dot3(a, b, dims=NN):
    return dot(a[0], b[0], dims) + dot(a[0], b[1], dims) + dot(a[1], b[0], dims)


def ones_where(mask):
    return jnp.where(mask, 1.0, 0.0).astype(BF)


def call(body, out_shape, scratch, args, smem=0, hbm=0, keep=None, vmem=20):
    spaces = [pltpu.SMEM] * smem + [pltpu.HBM] * hbm
    spaces += [pltpu.VMEM] * (len(args) - smem - hbm)
    if hbm:
        fetched = [pltpu.with_memory_space_constraint(a, pltpu.HBM) for a in args[smem : smem + hbm]]
        args = tuple(args[:smem]) + tuple(fetched) + tuple(args[smem + hbm :])
        scratch = [pltpu.SemaphoreType.DMA((hbm,))] + [pltpu.VMEM(a.shape, a.dtype) for a in fetched[:keep]] + scratch
    return pl.pallas_call(
        body,
        out_shape=out_shape,
        in_specs=[pl.BlockSpec(memory_space=space) for space in spaces],
        out_specs=jax.tree.map(lambda _: pl.BlockSpec(memory_space=pltpu.VMEM), out_shape),
        scratch_shapes=scratch,
        compiler_params=pltpu.CompilerParams(vmem_limit_bytes=vmem << 20),
    )(*args)


def fetch(sources, places, sems):
    copies = [pltpu.make_async_copy(a, b, sems.at[i]) for i, (a, b) in enumerate(zip(sources, places))]
    for copy in copies:
        copy.start()
    return copies


def slot_of(rel, core):
    return (rel >> 1) + jnp.where((rel & 1) == core, 0, 8)


def gather_body(
    core_ref, cols, rows_ref, head, tail,
    hv_hi, hv_lo, hvt_hi, hvt_lo, tv, n_hi, n_lo, rank_col, meta, head_hl, tail_hl, head_col,
):
    core = core_ref[0]
    width = head.shape[1]
    triples = cols.shape[0]
    high, low = split(head[...])
    head_hl[:, :width] = high
    head_hl[:, width:] = low
    high, low = split(tail[...])
    tail_hl[:, :width] = high
    tail_hl[:, width:] = low
    step = 256
    chunks = triples // step
    lanes = lax.broadcasted_iota(jnp.int32, (1, triples), 1)
    sublanes = lax.broadcasted_iota(jnp.int32, (step, 1), 0)
    key_row = slot_of(rows_ref[2:3, :], core) * triples + lanes
    rank_row = jnp.zeros((1, triples), F32)
    for i in range(chunks):
        part = slice(i * step, (i + 1) * step)
        key_col = slot_of(cols[part, 2:3], core) * triples + sublanes + i * step
        rank_row += jnp.sum(jnp.where(key_col < key_row, 1.0, 0.0), axis=0, keepdims=True)
        rank = jnp.sum(jnp.where(key_row < key_col, 1.0, 0.0), axis=1, keepdims=True)
        rank_col[part, :] = rank.astype(jnp.int32)
    rank_row = rank_row.astype(jnp.int32)
    head_row = jnp.zeros((1, triples), F32)
    head_ids = rows_ref[0:1, :].astype(F32)
    for i in range(chunks):
        part = slice(i * step, (i + 1) * step)
        here = rank_col[part, :] == lanes
        head_row += jnp.sum(jnp.where(here, cols[part, 0:1].astype(F32), 0.0), axis=0, keepdims=True)
        here = sublanes + i * step == rank_row
        head_col[part, :] = jnp.sum(jnp.where(here, head_ids, 0.0), axis=1, keepdims=True).astype(jnp.int32)
    meta[0:1, :] = rank_row
    meta[1:2, :] = head_row.astype(jnp.int32)

    def chunk(i, carry):
        rows = pl.ds(pl.multiple_of(i * step, step), step)
        part = cols[rows, :]

        def pick(index, table):
            ids = lax.broadcasted_iota(jnp.int32, (step, table.shape[0]), 1)
            return dot(ones_where(index == ids), table[...])

        both = pick(head_col[rows, :], head_hl)
        high, low = both[:, :width], both[:, width:]
        hv_hi[rows, :] = high.astype(BF)
        hv_lo[rows, :] = low.astype(BF)
        hvt_hi[:, rows] = jnp.transpose(high).astype(BF)
        hvt_lo[:, rows] = jnp.transpose(low).astype(BF)
        both = pick(part[:, 1:2], tail_hl)
        tv[rows, :] = both[:, :width] + both[:, width:]
        both = pick(part[:, 3:4], tail_hl)
        n_hi[rows, :] = both[:, :width].astype(BF)
        n_lo[rows, :] = both[:, width:].astype(BF)
        return carry

    lax.fori_loop(0, chunks, chunk, 0)


def order_of(piece):
    return (piece % 4) * 2 + piece // 4


def slot_order(slot):
    return (slot & 1) * 4 + (slot >> 1)


def split_rels(halves, r_hi, r_lo, copies=None):
    for half, mats in enumerate(halves):
        chips, deep = mats.shape[:2]
        if copies:
            copies[half].wait()
        for slot in range(8):
            for piece in range(chips // 8):
                high, low = split(mats[order_of(piece) * 8 + slot_order(slot)])
                start = (half * chips + slot * (chips // 8) + piece) * deep
                r_hi[start : start + deep, :] = high
                r_lo[start : start + deep, :] = low


def keep_half(half, count, first, last, slot):
    if half is None:
        return last, slot
    if half == 0:
        return jnp.where(slot < count, last, first), jnp.minimum(slot, count - 1)
    return jnp.where(slot >= count, last, first), jnp.maximum(slot - count, 0)


def visits(segs, tile, total, one, low=0, high=None):
    group = 4

    def some(g, carry):
        for k in range(group):
            v = g * group + k
            first = segs[0, v]
            one(pl.multiple_of(jnp.minimum(first // tile, total // tile - 1) * tile, tile), first, segs[1, v], segs[2, v])
        return carry

    lax.fori_loop(low, segs.shape[1] // group if high is None else high, some, 0)


def by_relation(segs, a_hi, a_lo, r_hi, r_lo, out, dims, half=None, low=0, high=None):
    width = r_hi.shape[1]
    tile = 128

    def one(start, first, last, slot):
        last, slot = keep_half(half, r_hi.shape[0] // width, first, last, slot)
        rows = pl.ds(start, tile)
        place = start + lax.broadcasted_iota(jnp.int32, (tile, 1), 0)
        mask = ones_where((place >= first) & (place < last))
        top = a_hi[rows, :] * mask
        both = jnp.concatenate([top, a_lo[rows, :] * mask], axis=0)
        mat = pl.ds(pl.multiple_of(slot * width, width), width)
        main = dot(both, r_hi[mat, :], dims)
        out[rows, :] += main[:tile] + main[tile:] + dot(top, r_lo[mat, :], dims)

    visits(segs, tile, out.shape[0], one, low, high)


def query_body(
    segs, bounds, own_at, hv_hi_at, hv_lo_at, tv_at, n_hi_at, n_lo_at, rank_at,
    query, hv_hi, hv_lo, tv, n_hi, n_lo, rank_col, sems, own, r_hi, r_lo,
):
    sources = (own_at, hv_hi_at, hv_lo_at, tv_at, n_hi_at, n_lo_at, rank_at)
    copies = fetch(sources, (own, hv_hi, hv_lo, tv, n_hi, n_lo, rank_col), sems)
    query[...] = jnp.zeros_like(query)
    split_rels((own,), r_hi, r_lo, copies)
    copies[1].wait()
    copies[2].wait()
    by_relation(segs, hv_hi, hv_lo, r_hi, r_lo, query, NN, 0, bounds[0, 0], bounds[0, 1])
    for copy in copies[3:]:
        copy.wait()


def factor_body(
    segs, bounds, partial, hv_hi, hv_lo, tv, n_hi, n_lo, rank_col, other, meta,
    f_hi, f_lo, d_hl, r_hi, r_lo, query, pair, f_hl,
):
    width = other.shape[2]
    triples = tv.shape[0]
    batch = triples // 2
    query[...] = partial[...]
    split_rels((other,), r_hi, r_lo)
    by_relation(segs, hv_hi, hv_lo, r_hi, r_lo, query, NN, 1, bounds[1, 0], bounds[1, 1])
    high, low = split(query[...])
    pair[:, :width] = high
    pair[:, width:] = low
    for s in range(2):
        rows = slice(s * batch, (s + 1) * batch)
        ids = lax.broadcasted_iota(jnp.int32, (batch, triples), 1)
        both = dot(ones_where(rank_col[rows, :] == ids), pair[...])
        high, low = both[:, :width], both[:, width:]
        q = high + low
        q2 = (high.astype(BF), low.astype(BF))
        n2 = (n_hi[rows, :], n_lo[rows, :])
        weights = split(jax.nn.sigmoid(dot3(q2, n2, NT)) * (1.0 / batch))
        vec = tv[rows, :]
        coef = -jax.nn.sigmoid(-jnp.sum(q * vec, axis=1, keepdims=True))
        high, low = split(coef * vec + dot3(weights, n2))
        f_hl[rows, :width] = high
        f_hl[rows, width:] = low
        high, low = split(coef * q)
        d_hl[rows, :width] = high
        d_hl[rows, width:] = low
        high, low = split(dot3(weights, q2, TN))
        below = slice(triples + s * batch, triples + (s + 1) * batch)
        d_hl[below, :width] = high
        d_hl[below, width:] = low
    rank_row = meta[0:1, :]
    for s in range(2):
        rows = slice(s * batch, (s + 1) * batch)
        ids = lax.broadcasted_iota(jnp.int32, (batch, triples), 0) + s * batch
        both = dot(ones_where(ids == rank_row), f_hl[...])
        f_hi[rows, :] = both[:, :width].astype(BF)
        f_lo[rows, :] = both[:, width:].astype(BF)


def rel_body(half, segs, bounds, hvt_hi, hvt_lo, f_hi, f_lo, out):
    width = f_hi.shape[1]
    tile = 256
    chips, deep = out.shape[:2]
    pieces = width // deep
    count = chips // pieces
    out[...] = jnp.zeros_like(out)

    def one(start, first, last, slot):
        part = pl.ds(start, tile)
        last, slot = keep_half(half, count, first, last, slot)
        place = start + lax.broadcasted_iota(jnp.int32, (1, tile), 1)
        mask = ones_where((place >= first) & (place < last))
        high = hvt_hi[:, part] * mask
        both = jnp.concatenate([high, hvt_lo[:, part] * mask], axis=0)
        main = dot(both, f_hi[part, :])
        total = main[:width] + main[width:] + dot(high, f_lo[part, :])
        for piece in range(pieces):
            out[slot * pieces + piece] += total[piece * deep : (piece + 1) * deep]

    visits(segs, tile, f_hi.shape[0], one, bounds[half, 0], bounds[half, 1])


def head_body(
    segs, f_hi_at, f_lo_at, own_at, other_at, meta, head_grad, sems, f_hi, f_lo, own, other, r_hi, r_lo, through, th_hl
):
    copies = fetch((f_hi_at, f_lo_at, own_at, other_at), (f_hi, f_lo, own, other), sems)
    split_rels((own, other), r_hi, r_lo, copies[2:])
    for copy in copies[:2]:
        copy.wait()
    head_part(segs, meta, f_hi, f_lo, head_grad, r_hi, r_lo, through, th_hl)


def tail_body(half, core_ref, rows_ref, d_hl, out):
    core = core_ref[0]
    width = out.shape[1]
    ids = jnp.concatenate([rows_ref[1:2, :], rows_ref[3:4, :]], axis=1)
    step = 512
    block = 128
    parity = core if half == 0 else 1 - core

    def chunk(i, carry):
        place = i * step + lax.broadcasted_iota(jnp.int32, (step, ids.shape[1]), 0)
        row = (place >> 7) * (2 * block) + parity * block + (place & (block - 1))
        both = dot(ones_where(row == ids), d_hl[...])
        rows = pl.ds(pl.multiple_of(i * step, step), step)
        out[rows, :] = both[:, :width] + both[:, width:]
        return carry

    lax.fori_loop(0, out.shape[0] // step, chunk, 0)


def head_part(segs, meta, f_hi, f_lo, out, r_hi, r_lo, through, th_hl):
    width = out.shape[1]
    through[...] = jnp.zeros_like(through)
    by_relation(segs, f_hi, f_lo, r_hi, r_lo, through, NT)
    high, low = split(through[...])
    th_hl[:, :width] = high
    th_hl[:, width:] = low
    ids = meta[1:2, :]
    place = lax.broadcasted_iota(jnp.int32, (out.shape[0], ids.shape[1]), 0)
    both = dot(ones_where(place == ids), th_hl[...])
    out[...] = both[:, :width] + both[:, width:]


def shape(*dims, dtype=F32):
    return jax.ShapeDtypeStruct(dims, dtype)


def half_bounds(segs, starts):
    middle = jnp.sum((segs[0] < starts[starts.shape[0] // 2]).astype(jnp.int32))
    end = jnp.full_like(middle, segs.shape[1] // 4)
    return jnp.stack([jnp.stack([jnp.zeros_like(middle), (middle + 3) // 4]), jnp.stack([middle // 4, end])])


def after(value, earlier):
    return lax.optimization_barrier((value, earlier))[0]


def exchange(value, axes):
    pieces = value.reshape(lax.axis_size(axes), -1, value.shape[-1])
    return lax.all_to_all(pieces, axes, split_axis=0, concat_axis=0)


def segments(starts, tile, total):
    edges = jnp.concatenate([jnp.arange(0, total, tile, dtype=jnp.int32), starts[1:]])
    count = edges.shape[0]
    place = jnp.arange(count)
    ahead = (edges[None, :] < edges[:, None]) | (
        (edges[None, :] == edges[:, None]) & (place[None, :] < place[:, None])
    )
    rank = jnp.sum(ahead.astype(jnp.int32), axis=1)
    padded = -(-count // 4) * 4
    at = jnp.arange(padded + 1)
    ordered = jnp.sum(jnp.where(rank[None, :] == at[:, None], edges[None, :], 0), axis=1)
    ordered = jnp.where(at < count, ordered, total)
    first = ordered[:padded]
    slot = jnp.sum((starts[None, 1:] <= first[:, None]).astype(jnp.int32), axis=1)
    return jnp.stack([first, ordered[1:], slot]).astype(jnp.int32)


def permute_sum(value, axis, behind=None):
    devices = lax.axis_size(axis)
    me = lax.axis_index(axis)
    total = lax.dynamic_index_in_dim(value, me, 0, keepdims=False)
    if behind is not None:
        total = after(total, behind)
    for k in range(1, devices):
        piece = lax.dynamic_index_in_dim(value, me ^ k, 0, keepdims=False)
        total += lax.ppermute(piece, axis, [(i, i ^ k) for i in range(devices)])
    return total


def per_device(head_emb, tail_emb, relations, head_index, tail_index, rel_index, neg_index):
    width = relations.shape[1]
    heads = head_emb[0]
    tails = tail_emb[0]
    batch = head_index.shape[4]
    triples = 2 * batch
    index = jnp.stack([a[0, 0, :, 0] for a in (head_index, tail_index, rel_index, neg_index)], axis=1)
    behind = lax.axis_size(TAIL)
    next_index = lax.ppermute(index[1], TAIL, [(i, (i - 1) % behind) for i in range(behind)])
    core = lax.axis_index("c").astype(jnp.int32).reshape(1)

    chips = lax.axis_size(CHIPS)
    spread = jnp.broadcast_to(relations[None], (chips,) + relations.shape)
    spread, next_index = lax.optimization_barrier((spread, next_index))
    rows = jnp.concatenate([index[0], next_index], axis=1)
    cols = jnp.transpose(rows)
    own = lax.all_to_all(spread, CHIPS, split_axis=0, concat_axis=0)
    wide = shape(triples, width, dtype=BF)
    high = shape(width, triples, dtype=BF)
    gathered = call(
        gather_body,
        [wide, wide, high, high, shape(triples, width), wide, wide]
        + [shape(triples, 1, dtype=jnp.int32), shape(2, triples, dtype=jnp.int32)],
        [
            pltpu.VMEM((heads.shape[0], 2 * width), BF),
            pltpu.VMEM((tails.shape[0], 2 * width), BF),
            pltpu.VMEM((triples, 1), jnp.int32),
        ],
        (core, cols, rows, heads, tails),
        smem=1,
    )
    hv_hi, hv_lo, hvt_hi, hvt_lo, tv, n_hi, n_lo, rank_col, meta = gathered
    slots = slot_of(after(rows[2], meta), core)
    rel_count = 2 * lax.axis_size(HEAD_CHIPS)
    starts = jnp.sum((slots[None, :] < jnp.arange(rel_count)[:, None]).astype(jnp.int32), axis=1)
    by_row = segments(starts, 128, triples)
    by_column = segments(starts, 256, triples)
    row_bounds = half_bounds(by_row, starts)
    bounds = half_bounds(by_column, starts)
    meta, own, by_row, row_bounds, by_column, bounds = lax.optimization_barrier(
        (meta, own, by_row, row_bounds, by_column, bounds)
    )
    other = lax.ppermute(own, "c", SWAP)
    half_rows = own.shape[0] * own.shape[1]
    half_scratch = [pltpu.VMEM((half_rows, width), BF)] * 2
    plain = shape(triples, width)
    ready = call(
        query_body,
        [plain, wide, wide, plain, wide, wide, shape(triples, 1, dtype=jnp.int32)],
        half_scratch,
        (by_row, row_bounds, own, hv_hi, hv_lo, tv, n_hi, n_lo, rank_col),
        smem=2,
        hbm=7,
        keep=1,
    )
    f_hi, f_lo, d_hl = call(
        factor_body,
        [wide, wide, shape(2 * triples, 2 * width, dtype=BF)],
        half_scratch + [pltpu.VMEM((triples, width), F32)] + [pltpu.VMEM((triples, 2 * width), BF)] * 2,
        (by_row, row_bounds, *ready, other, meta),
        smem=2,
    )

    def rel_part(half, bounds):
        out = shape(*own.shape)
        args = (by_column, bounds, hvt_hi, hvt_lo, f_hi, f_lo)
        return call(functools.partial(rel_body, half), out, [], args, smem=2)

    def tail_part(half, core):
        out = shape(tails.shape[0] // 2, width)
        return call(functools.partial(tail_body, half), out, [], (core, rows, d_hl), smem=1)

    rel_other = rel_part(1, bounds)
    rel_came = lax.ppermute(rel_other, "c", SWAP)
    rel_own = rel_part(0, after(bounds, rel_other))
    tail_theirs = tail_part(1, after(core, rel_own))
    tail_came = lax.ppermute(tail_theirs, "c", SWAP)
    rel_sum = rel_own + rel_came
    rel_pieces = exchange(rel_sum, OWNERS)

    tail_mine = tail_part(0, after(core, rel_sum))
    head_grad = call(
        head_body,
        shape(*heads.shape),
        [pltpu.VMEM((2 * half_rows, width), BF)] * 2
        + [pltpu.VMEM((triples, width), F32), pltpu.VMEM((triples, 2 * width), BF)],
        (after(by_row, tail_mine), f_hi, f_lo, own, other, meta),
        smem=1,
        hbm=4,
        vmem=32,
    )
    pieces = head_grad.reshape(lax.axis_size("zl"), lax.axis_size("x"), -1, width)
    pieces = permute_sum(jnp.swapaxes(pieces, 0, 1), "x")
    tail_sum = after(tail_mine + tail_came, (head_grad, rel_pieces))
    tail_share = jnp.sum(exchange(tail_sum, HEAD_CHIPS), axis=0)
    rel_share = jnp.sum(rel_pieces, axis=0)
    head_share = permute_sum(pieces, "zl", rel_share)
    return (head_share[None], tail_share[None], rel_share)


def solution(mesh):
    fine = Mesh(mesh.devices.reshape(4, 2, 2, 2, 4), ("y", "zh", "c", "zl", "x"))
    placed = (
        P(HEAD, None, None),
        P(TAIL, None, None),
        P(HEAD + TAIL, None),
        P(HEAD, TAIL, None, None, None),
        P(HEAD, TAIL, None, None, None),
        P(HEAD, TAIL, None, None, None),
        P(HEAD, TAIL, None, None, None),
    )
    return jax.shard_map(
        per_device,
        mesh=fine,
        in_specs=placed,
        out_specs=(P(HEAD, TAIL, None), P(TAIL, HEAD, None), P(HEAD + TAIL, None)),
        check_vma=False,
    )
```

```python
import functools

import jax
import jax.numpy as jnp
from jax import lax
from jax.experimental import pallas as pl
from jax.experimental.pallas import tpu as pltpu
from jax.sharding import Mesh, PartitionSpec as P

BF = jnp.bfloat16
F32 = jnp.float32
CHIPS = ("x", "zl", "zh", "y")
OWNERS = ("y", "zh", "zl", "x")
HEAD = ("y", "zh", "c")
HEAD_CHIPS = ("y", "zh")
TAIL = ("zl", "x")
SWAP = [(0, 1), (1, 0)]
NN = (((1,), (0,)), ((), ()))
NT = (((1,), (1,)), ((), ()))
TN = (((0,), (0,)), ((), ()))


def split(value):
    high = value.astype(BF)
    return high, (value - high.astype(F32)).astype(BF)


def dot(a, b, dims=NN):
    return lax.dot_general(a, b, dims, preferred_element_type=F32)


def dot3(a, b, dims=NN):
    return dot(a[0], b[0], dims) + dot(a[0], b[1], dims) + dot(a[1], b[0], dims)


def ones_where(mask):
    return jnp.where(mask, 1.0, 0.0).astype(BF)


def call(body, out_shape, scratch, args, smem=0, hbm=0, keep=None, vmem=20):
    spaces = [pltpu.SMEM] * smem + [pltpu.HBM] * hbm
    spaces += [pltpu.VMEM] * (len(args) - smem - hbm)
    if hbm:
        fetched = [pltpu.with_memory_space_constraint(a, pltpu.HBM) for a in args[smem : smem + hbm]]
        args = tuple(args[:smem]) + tuple(fetched) + tuple(args[smem + hbm :])
        scratch = [pltpu.SemaphoreType.DMA((hbm,))] + [pltpu.VMEM(a.shape, a.dtype) for a in fetched[:keep]] + scratch
    return pl.pallas_call(
        body,
        out_shape=out_shape,
        in_specs=[pl.BlockSpec(memory_space=space) for space in spaces],
        out_specs=jax.tree.map(lambda _: pl.BlockSpec(memory_space=pltpu.VMEM), out_shape),
        scratch_shapes=scratch,
        compiler_params=pltpu.CompilerParams(vmem_limit_bytes=vmem << 20),
    )(*args)


def fetch(sources, places, sems):
    copies = [pltpu.make_async_copy(a, b, sems.at[i]) for i, (a, b) in enumerate(zip(sources, places))]
    for copy in copies:
        copy.start()
    return copies


def slot_of(rel, core):
    return (rel >> 1) + jnp.where((rel & 1) == core, 0, 8)


def gather_body(
    core_ref, cols, rows_ref, head, tail,
    hv_hi, hv_lo, hvt_hi, hvt_lo, tv, n_hi, n_lo, rank_col, meta, head_hl, tail_hl, head_col,
):
    core = core_ref[0]
    width = head.shape[1]
    triples = cols.shape[0]
    high, low = split(head[...])
    head_hl[:, :width] = high
    head_hl[:, width:] = low
    high, low = split(tail[...])
    tail_hl[:, :width] = high
    tail_hl[:, width:] = low
    step = 256
    chunks = triples // step
    lanes = lax.broadcasted_iota(jnp.int32, (1, triples), 1)
    sublanes = lax.broadcasted_iota(jnp.int32, (step, 1), 0)
    key_row = slot_of(rows_ref[2:3, :], core) * triples + lanes
    rank_row = jnp.zeros((1, triples), F32)
    for i in range(chunks):
        part = slice(i * step, (i + 1) * step)
        key_col = slot_of(cols[part, 2:3], core) * triples + sublanes + i * step
        rank_row += jnp.sum(jnp.where(key_col < key_row, 1.0, 0.0), axis=0, keepdims=True)
        rank = jnp.sum(jnp.where(key_row < key_col, 1.0, 0.0), axis=1, keepdims=True)
        rank_col[part, :] = rank.astype(jnp.int32)
    rank_row = rank_row.astype(jnp.int32)
    head_row = jnp.zeros((1, triples), F32)
    head_ids = rows_ref[0:1, :].astype(F32)
    for i in range(chunks):
        part = slice(i * step, (i + 1) * step)
        here = rank_col[part, :] == lanes
        head_row += jnp.sum(jnp.where(here, cols[part, 0:1].astype(F32), 0.0), axis=0, keepdims=True)
        here = sublanes + i * step == rank_row
        head_col[part, :] = jnp.sum(jnp.where(here, head_ids, 0.0), axis=1, keepdims=True).astype(jnp.int32)
    meta[0:1, :] = rank_row
    meta[1:2, :] = head_row.astype(jnp.int32)

    def chunk(i, carry):
        rows = pl.ds(pl.multiple_of(i * step, step), step)
        part = cols[rows, :]

        def pick(index, table):
            ids = lax.broadcasted_iota(jnp.int32, (step, table.shape[0]), 1)
            return dot(ones_where(index == ids), table[...])

        both = pick(head_col[rows, :], head_hl)
        high, low = both[:, :width], both[:, width:]
        hv_hi[rows, :] = high.astype(BF)
        hv_lo[rows, :] = low.astype(BF)
        hvt_hi[:, rows] = jnp.transpose(high).astype(BF)
        hvt_lo[:, rows] = jnp.transpose(low).astype(BF)
        both = pick(part[:, 1:2], tail_hl)
        tv[rows, :] = both[:, :width] + both[:, width:]
        both = pick(part[:, 3:4], tail_hl)
        n_hi[rows, :] = both[:, :width].astype(BF)
        n_lo[rows, :] = both[:, width:].astype(BF)
        return carry

    lax.fori_loop(0, chunks, chunk, 0)


def order_of(piece):
    return (piece % 4) * 2 + piece // 4


def slot_order(slot):
    return (slot & 1) * 4 + (slot >> 1)


def split_rels(halves, r_hi, r_lo, copies=None):
    for half, mats in enumerate(halves):
        chips, deep = mats.shape[:2]
        if copies:
            copies[half].wait()
        for slot in range(8):
            for piece in range(chips // 8):
                high, low = split(mats[order_of(piece) * 8 + slot_order(slot)])
                start = (half * chips + slot * (chips // 8) + piece) * deep
                r_hi[start : start + deep, :] = high
                r_lo[start : start + deep, :] = low


def keep_half(half, count, first, last, slot):
    if half is None:
        return last, slot
    if half == 0:
        return jnp.where(slot < count, last, first), jnp.minimum(slot, count - 1)
    return jnp.where(slot >= count, last, first), jnp.maximum(slot - count, 0)


def visits(segs, tile, total, one, low=0, high=None):
    group = 4

    def some(g, carry):
        for k in range(group):
            v = g * group + k
            first = segs[0, v]
            one(pl.multiple_of(jnp.minimum(first // tile, total // tile - 1) * tile, tile), first, segs[1, v], segs[2, v])
        return carry

    lax.fori_loop(low, segs.shape[1] // group if high is None else high, some, 0)


def by_relation(segs, a_hi, a_lo, r_hi, r_lo, out, dims, half=None, low=0, high=None):
    width = r_hi.shape[1]
    tile = 128

    def one(start, first, last, slot):
        last, slot = keep_half(half, r_hi.shape[0] // width, first, last, slot)
        rows = pl.ds(start, tile)
        place = start + lax.broadcasted_iota(jnp.int32, (tile, 1), 0)
        mask = ones_where((place >= first) & (place < last))
        top = a_hi[rows, :] * mask
        both = jnp.concatenate([top, a_lo[rows, :] * mask], axis=0)
        mat = pl.ds(pl.multiple_of(slot * width, width), width)
        main = dot(both, r_hi[mat, :], dims)
        out[rows, :] += main[:tile] + main[tile:] + dot(top, r_lo[mat, :], dims)

    visits(segs, tile, out.shape[0], one, low, high)


def query_body(
    segs, bounds, own_at, hv_hi_at, hv_lo_at, tv_at, n_hi_at, n_lo_at, rank_at,
    query, hv_hi, hv_lo, tv, n_hi, n_lo, rank_col, sems, own, r_hi, r_lo,
):
    sources = (own_at, hv_hi_at, hv_lo_at, tv_at, n_hi_at, n_lo_at, rank_at)
    copies = fetch(sources, (own, hv_hi, hv_lo, tv, n_hi, n_lo, rank_col), sems)
    query[...] = jnp.zeros_like(query)
    split_rels((own,), r_hi, r_lo, copies)
    copies[1].wait()
    copies[2].wait()
    by_relation(segs, hv_hi, hv_lo, r_hi, r_lo, query, NN, 0, bounds[0, 0], bounds[0, 1])
    for copy in copies[3:]:
        copy.wait()


def factor_body(
    segs, bounds, partial, hv_hi, hv_lo, tv, n_hi, n_lo, rank_col, other, meta,
    f_hi, f_lo, d_hl, r_hi, r_lo, query, pair, f_hl,
):
    width = other.shape[2]
    triples = tv.shape[0]
    batch = triples // 2
    query[...] = partial[...]
    split_rels((other,), r_hi, r_lo)
    by_relation(segs, hv_hi, hv_lo, r_hi, r_lo, query, NN, 1, bounds[1, 0], bounds[1, 1])
    high, low = split(query[...])
    pair[:, :width] = high
    pair[:, width:] = low
    for s in range(2):
        rows = slice(s * batch, (s + 1) * batch)
        ids = lax.broadcasted_iota(jnp.int32, (batch, triples), 1)
        both = dot(ones_where(rank_col[rows, :] == ids), pair[...])
        high, low = both[:, :width], both[:, width:]
        q = high + low
        q2 = (high.astype(BF), low.astype(BF))
        both_q = both.astype(BF)
        n2 = (n_hi[rows, :], n_lo[rows, :])
        weights = split(jax.nn.sigmoid(dot3(q2, n2, NT)) * (1.0 / batch))
        vec = tv[rows, :]
        coef = -jax.nn.sigmoid(-jnp.sum(q * vec, axis=1, keepdims=True))
        high, low = split(coef * vec + dot3(weights, n2))
        f_hl[rows, :width] = high
        f_hl[rows, width:] = low
        high, low = split(coef * q)
        d_hl[rows, :width] = high
        d_hl[rows, width:] = low
        wide = dot(weights[0], both_q, TN)
        high, low = split(wide[:, :width] + wide[:, width:] + dot(weights[1], q2[0], TN))
        below = slice(triples + s * batch, triples + (s + 1) * batch)
        d_hl[below, :width] = high
        d_hl[below, width:] = low
    rank_row = meta[0:1, :]
    for s in range(2):
        rows = slice(s * batch, (s + 1) * batch)
        ids = lax.broadcasted_iota(jnp.int32, (batch, triples), 0) + s * batch
        both = dot(ones_where(ids == rank_row), f_hl[...])
        f_hi[rows, :] = both[:, :width].astype(BF)
        f_lo[rows, :] = both[:, width:].astype(BF)


def rel_body(half, segs, bounds, hvt_hi, hvt_lo, f_hi, f_lo, out):
    width = f_hi.shape[1]
    tile = 256
    chips, deep = out.shape[:2]
    pieces = width // deep
    count = chips // pieces
    out[...] = jnp.zeros_like(out)

    def one(start, first, last, slot):
        part = pl.ds(start, tile)
        last, slot = keep_half(half, count, first, last, slot)
        place = start + lax.broadcasted_iota(jnp.int32, (1, tile), 1)
        mask = ones_where((place >= first) & (place < last))
        high = hvt_hi[:, part] * mask
        both = jnp.concatenate([high, hvt_lo[:, part] * mask], axis=0)
        main = dot(both, f_hi[part, :])
        total = main[:width] + main[width:] + dot(high, f_lo[part, :])
        for piece in range(pieces):
            out[slot * pieces + piece] += total[piece * deep : (piece + 1) * deep]

    visits(segs, tile, f_hi.shape[0], one, bounds[half, 0], bounds[half, 1])


def head_body(
    segs, f_hi_at, f_lo_at, own_at, other_at, meta, head_grad, sems, f_hi, f_lo, own, other, r_hi, r_lo, through, th_hl
):
    copies = fetch((f_hi_at, f_lo_at, own_at, other_at), (f_hi, f_lo, own, other), sems)
    split_rels((own, other), r_hi, r_lo, copies[2:])
    for copy in copies[:2]:
        copy.wait()
    head_part(segs, meta, f_hi, f_lo, head_grad, r_hi, r_lo, through, th_hl)


def tail_body(half, core_ref, rows_ref, d_hl, out):
    core = core_ref[0]
    width = out.shape[1]
    ids = jnp.concatenate([rows_ref[1:2, :], rows_ref[3:4, :]], axis=1)
    step = 512
    block = 128
    parity = core if half == 0 else 1 - core

    def chunk(i, carry):
        place = i * step + lax.broadcasted_iota(jnp.int32, (step, ids.shape[1]), 0)
        row = (place >> 7) * (2 * block) + parity * block + (place & (block - 1))
        both = dot(ones_where(row == ids), d_hl[...])
        rows = pl.ds(pl.multiple_of(i * step, step), step)
        out[rows, :] = both[:, :width] + both[:, width:]
        return carry

    lax.fori_loop(0, out.shape[0] // step, chunk, 0)


def head_part(segs, meta, f_hi, f_lo, out, r_hi, r_lo, through, th_hl):
    width = out.shape[1]
    through[...] = jnp.zeros_like(through)
    by_relation(segs, f_hi, f_lo, r_hi, r_lo, through, NT)
    high, low = split(through[...])
    th_hl[:, :width] = high
    th_hl[:, width:] = low
    ids = meta[1:2, :]
    place = lax.broadcasted_iota(jnp.int32, (out.shape[0], ids.shape[1]), 0)
    both = dot(ones_where(place == ids), th_hl[...])
    out[...] = both[:, :width] + both[:, width:]


def shape(*dims, dtype=F32):
    return jax.ShapeDtypeStruct(dims, dtype)


def half_bounds(segs, starts):
    middle = jnp.sum((segs[0] < starts[starts.shape[0] // 2]).astype(jnp.int32))
    end = jnp.full_like(middle, segs.shape[1] // 4)
    return jnp.stack([jnp.stack([jnp.zeros_like(middle), (middle + 3) // 4]), jnp.stack([middle // 4, end])])


def after(value, earlier):
    return lax.optimization_barrier((value, earlier))[0]


def exchange(value, axes):
    pieces = value.reshape(lax.axis_size(axes), -1, value.shape[-1])
    return lax.all_to_all(pieces, axes, split_axis=0, concat_axis=0)


def segments(starts, tile, total):
    edges = jnp.concatenate([jnp.arange(0, total, tile, dtype=jnp.int32), starts[1:]])
    count = edges.shape[0]
    place = jnp.arange(count)
    ahead = (edges[None, :] < edges[:, None]) | (
        (edges[None, :] == edges[:, None]) & (place[None, :] < place[:, None])
    )
    rank = jnp.sum(ahead.astype(jnp.int32), axis=1)
    padded = -(-count // 4) * 4
    at = jnp.arange(padded + 1)
    ordered = jnp.sum(jnp.where(rank[None, :] == at[:, None], edges[None, :], 0), axis=1)
    ordered = jnp.where(at < count, ordered, total)
    first = ordered[:padded]
    slot = jnp.sum((starts[None, 1:] <= first[:, None]).astype(jnp.int32), axis=1)
    return jnp.stack([first, ordered[1:], slot]).astype(jnp.int32)


def permute_sum(value, axis, behind=None):
    devices = lax.axis_size(axis)
    me = lax.axis_index(axis)
    total = lax.dynamic_index_in_dim(value, me, 0, keepdims=False)
    if behind is not None:
        total = after(total, behind)
    for k in range(1, devices):
        piece = lax.dynamic_index_in_dim(value, me ^ k, 0, keepdims=False)
        total += lax.ppermute(piece, axis, [(i, i ^ k) for i in range(devices)])
    return total


def per_device(head_emb, tail_emb, relations, head_index, tail_index, rel_index, neg_index):
    width = relations.shape[1]
    heads = head_emb[0]
    tails = tail_emb[0]
    batch = head_index.shape[4]
    triples = 2 * batch
    index = jnp.stack([a[0, 0, :, 0] for a in (head_index, tail_index, rel_index, neg_index)], axis=1)
    behind = lax.axis_size(TAIL)
    next_index = lax.ppermute(index[1], TAIL, [(i, (i - 1) % behind) for i in range(behind)])
    core = lax.axis_index("c").astype(jnp.int32).reshape(1)

    chips = lax.axis_size(CHIPS)
    spread = jnp.broadcast_to(relations[None], (chips,) + relations.shape)
    spread, next_index = lax.optimization_barrier((spread, next_index))
    rows = jnp.concatenate([index[0], next_index], axis=1)
    cols = jnp.transpose(rows)
    own = lax.all_to_all(spread, CHIPS, split_axis=0, concat_axis=0)
    slots = slot_of(rows[2], core)
    rel_count = 2 * lax.axis_size(HEAD_CHIPS)
    starts = jnp.sum((slots[None, :] < jnp.arange(rel_count)[:, None]).astype(jnp.int32), axis=1)
    by_row = segments(starts, 128, triples)
    by_column = segments(starts, 256, triples)
    row_bounds = half_bounds(by_row, starts)
    bounds = half_bounds(by_column, starts)
    wide = shape(triples, width, dtype=BF)
    high = shape(width, triples, dtype=BF)
    gathered = call(
        gather_body,
        [wide, wide, high, high, shape(triples, width), wide, wide]
        + [shape(triples, 1, dtype=jnp.int32), shape(2, triples, dtype=jnp.int32)],
        [
            pltpu.VMEM((heads.shape[0], 2 * width), BF),
            pltpu.VMEM((tails.shape[0], 2 * width), BF),
            pltpu.VMEM((triples, 1), jnp.int32),
        ],
        (core, cols, rows, heads, tails),
        smem=1,
    )
    hv_hi, hv_lo, hvt_hi, hvt_lo, tv, n_hi, n_lo, rank_col, meta = gathered
    meta, own, by_row, row_bounds, by_column, bounds = lax.optimization_barrier(
        (meta, own, by_row, row_bounds, by_column, bounds)
    )
    other = lax.ppermute(own, "c", SWAP)
    half_rows = own.shape[0] * own.shape[1]
    half_scratch = [pltpu.VMEM((half_rows, width), BF)] * 2
    plain = shape(triples, width)
    ready = call(
        query_body,
        [plain, wide, wide, plain, wide, wide, shape(triples, 1, dtype=jnp.int32)],
        half_scratch,
        (by_row, row_bounds, own, hv_hi, hv_lo, tv, n_hi, n_lo, rank_col),
        smem=2,
        hbm=7,
        keep=1,
    )
    f_hi, f_lo, d_hl = call(
        factor_body,
        [wide, wide, shape(2 * triples, 2 * width, dtype=BF)],
        half_scratch + [pltpu.VMEM((triples, width), F32)] + [pltpu.VMEM((triples, 2 * width), BF)] * 2,
        (by_row, row_bounds, *ready, other, meta),
        smem=2,
    )

    def rel_part(half, bounds):
        out = shape(*own.shape)
        args = (by_column, bounds, hvt_hi, hvt_lo, f_hi, f_lo)
        return call(functools.partial(rel_body, half), out, [], args, smem=2)

    def tail_part(half, core):
        out = shape(tails.shape[0] // 2, width)
        return call(functools.partial(tail_body, half), out, [], (core, rows, d_hl), smem=1)

    rel_other = rel_part(1, bounds)
    rel_came = lax.ppermute(rel_other, "c", SWAP)
    rel_own = rel_part(0, after(bounds, rel_other))
    tail_theirs = tail_part(1, after(core, rel_own))
    tail_came = lax.ppermute(tail_theirs, "c", SWAP)
    rel_sum = rel_own + rel_came
    rel_pieces = exchange(rel_sum, OWNERS)

    tail_mine = tail_part(0, after(core, rel_sum))
    head_grad = call(
        head_body,
        shape(*heads.shape),
        [pltpu.VMEM((2 * half_rows, width), BF)] * 2
        + [pltpu.VMEM((triples, width), F32), pltpu.VMEM((triples, 2 * width), BF)],
        (after(by_row, tail_mine), f_hi, f_lo, own, other, meta),
        smem=1,
        hbm=4,
        vmem=32,
    )
    pieces = head_grad.reshape(lax.axis_size("zl"), lax.axis_size("x"), -1, width)
    pieces = permute_sum(jnp.swapaxes(pieces, 0, 1), "x")
    tail_sum = after(tail_mine + tail_came, (head_grad, rel_pieces))
    tail_share = jnp.sum(exchange(tail_sum, HEAD_CHIPS), axis=0)
    rel_share = jnp.sum(rel_pieces, axis=0)
    head_share = permute_sum(pieces, "zl", rel_share)
    return (head_share[None], tail_share[None], rel_share)


def solution(mesh):
    fine = Mesh(mesh.devices.reshape(4, 2, 2, 2, 4), ("y", "zh", "c", "zl", "x"))
    placed = (
        P(HEAD, None, None),
        P(TAIL, None, None),
        P(HEAD + TAIL, None),
        P(HEAD, TAIL, None, None, None),
        P(HEAD, TAIL, None, None, None),
        P(HEAD, TAIL, None, None, None),
        P(HEAD, TAIL, None, None, None),
    )
    return jax.shard_map(
        per_device,
        mesh=fine,
        in_specs=placed,
        out_specs=(P(HEAD, TAIL, None), P(TAIL, HEAD, None), P(HEAD + TAIL, None)),
        check_vma=False,
    )
```
